32 devices in a mesh: grp: 2 (over y), dep: 4 (over z), hgt: 2 (over x), wid: 2 (over core).
Axes of the slice: x: 2, y: 2, z: 4, core: 2. Of those that a mesh axis runs over, the one named last changes fastest.
Arguments:
- features: bfloat16 [64, 8, 16, 256], P('grp', 'wid', 'dep', 'hgt'), parts along dimension 0, may hold values from -6 to 6
- cotangent: bfloat16 [64, 8, 16, 256], P('grp', 'wid', 'dep', 'hgt'), parts along dimension 0, may hold values from -6 to 6
- w_stem: bfloat16 [3, 3, 3, 32, 32], replicated, may hold values from -0.21875 to 0.21875
- w_middle: bfloat16 [3, 3, 3, 32, 64], replicated, may hold values from -0.21875 to 0.21875
- w_bottom: bfloat16 [3, 3, 3, 64, 128], replicated, may hold values from -0.15625 to 0.15625
- w_rise: bfloat16 [3, 3, 3, 192, 64], replicated, may hold values from -0.078125 to 0.078125
- w_final: bfloat16 [3, 3, 3, 96, 32], replicated, may hold values from -0.125 to 0.125
Outputs:
- output: bfloat16 [64, 8, 16, 256], P('grp', 'wid', 'dep', 'hgt'), parts along dimension 0
- grad_stem: float32 [6, 3, 3, 32, 32], P('grp'), parts along dimension 0
- grad_middle: float32 [6, 3, 3, 32, 64], P('grp'), parts along dimension 0
- grad_bottom: float32 [6, 3, 3, 64, 128], P('grp'), parts along dimension 0
- grad_rise: float32 [6, 3, 3, 192, 64], P('grp'), parts along dimension 0
- grad_final: float32 [6, 3, 3, 96, 32], P('grp'), parts along dimension 0
- half_grad: float32 [64, 4, 8, 128], P('grp', 'wid', 'dep', 'hgt'), parts along dimension 0
The draws below stay inside these ranges and needn't reach their ends.
There are 2 independent parts, one for each index of `grp`. The reference program is written for one: setup_inputs(seed, part) draws one part's arguments, and reference() takes and returns one part's arrays. A program takes and returns all parts, laid end to end along the dimension named above; an argument that names none is the same for every part. Nothing has to cross between parts.
All inputs are finite; a program needn't handle non-finite values.
Results may differ from the reference program's by a relative error of at most 0.012.
Values may be sent and summed in bfloat16 or wider, within the bound.
A program may use at most 128 MiB of HBM per device.

```python
import math
import jax
import jax.numpy as jnp
from jax import lax

F0 = 32
F1 = 64
F2 = 128
NW = 8
ND = 16
NH = 256


def block_scale(own_key, dims, split, least, top_value):
    factor_of, own = 1.0, jax.random.fold_in(own_key, 6)
    for axis_at, parts in split:
        draws = jnp.exp(jax.random.uniform(jax.random.fold_in(own, axis_at), (parts,), jnp.float32, least / len(split), top_value / len(split)))
        factor_of = factor_of * jnp.repeat(draws, dims[axis_at] // parts).reshape([-1 if axis == axis_at else 1 for axis in range(len(dims))])
    return factor_of


def gaussian(stream_key, dims, scale, limit, shards=(), held_as=jnp.bfloat16):
    gain = block_scale(stream_key, dims, shards, -0.22, 0.18) if shards else 1.0
    drawn = jax.random.normal(stream_key, dims, jnp.float32) * scale * gain
    return jnp.minimum(jnp.maximum(drawn, -limit), limit).astype(held_as)


def setup_inputs(seed: int = 0, part: int = 0) -> dict:
    keys = jax.random.split(jax.random.key(seed), 8)
    part_keys = jax.random.split(jax.random.fold_in(keys[7], part), 8)
    return {
        "features": gaussian(part_keys[0], (F0, NW, ND, NH), 1.0, 6.0, ((1, 2), (2, 4), (3, 2))),
        "cotangent": gaussian(part_keys[1], (F0, NW, ND, NH), 1.0, 6.0, ((1, 2), (2, 4), (3, 2))),
        "w_stem": gaussian(keys[2], (3, 3, 3, F0, F0), (27 * F0) ** -0.5, 0.21875),
        "w_middle": gaussian(keys[3], (3, 3, 3, F0, F1), (27 * F0) ** -0.5, 0.21875),
        "w_bottom": gaussian(keys[4], (3, 3, 3, F1, F2), (27 * F1) ** -0.5, 0.15625),
        "w_rise": gaussian(keys[5], (3, 3, 3, F2 + F1, F1), (27 * (F2 + F1)) ** -0.5, 0.078125),
        "w_final": gaussian(keys[6], (3, 3, 3, F1 + F0, F0), (27 * (F1 + F0)) ** -0.5, 0.125),
    }


def conv_valid(padded, weight):
    result = lax.conv_general_dilated(padded[None], weight, (1, 1, 1), 'VALID', dimension_numbers=('NCDHW', 'DHWIO', 'NCDHW'), preferred_element_type=jnp.float32)
    return result[0]

def conv_back(padded_grad, weight):
    flipped = jnp.swapaxes(weight[::-1, ::-1, ::-1], 3, 4)
    return conv_valid(padded_grad, flipped)

def weight_grad(padded, grad):
    span_w, span_d, span_h = (grad.shape[1], grad.shape[2], grad.shape[3])
    flat_grad = grad.reshape(grad.shape[0], -1)
    blocks = []
    for offset_a in range(3):
        for offset_b in range(3):
            for offset_c in range(3):
                window = padded[:, offset_a:offset_a + span_w, offset_b:offset_b + span_d, offset_c:offset_c + span_h]
                window = window.reshape(padded.shape[0], -1)
                blocks.append(lax.dot_general(window, flat_grad, (((1,), (1,)), ((), ())), preferred_element_type=jnp.float32))
    return jnp.stack(blocks).reshape(3, 3, 3, padded.shape[0], grad.shape[0])

def silu_act(value):
    return value * jax.nn.sigmoid(value)

def silu_slope(value):
    gating = jax.nn.sigmoid(value)
    return gating * (1.0 + value * (1.0 - gating))

def pool_mean(value):
    count_c, count_w, count_d, count_h = value.shape
    blocks = value.astype(jnp.float32).reshape(count_c, count_w // 2, 2, count_d // 2, 2, count_h // 2, 2)
    return lax.optimization_barrier(jnp.mean(blocks, axis=(2, 4, 6))).astype(jnp.bfloat16)

def pool_sum(value):
    count_c, count_w, count_d, count_h = value.shape
    return lax.optimization_barrier(jnp.sum(value.reshape(count_c, count_w // 2, 2, count_d // 2, 2, count_h // 2, 2), axis=(2, 4, 6)))

def upsample(value):
    count_c, count_w, count_d, count_h = value.shape
    spread = jnp.broadcast_to(value[:, :, None, :, None, :, None], (count_c, count_w, 2, count_d, 2, count_h, 2))
    return spread.reshape(count_c, 2 * count_w, 2 * count_d, 2 * count_h)

def pad_cells(value):
    return jnp.pad(value, ((0, 0), (1, 1), (1, 1), (1, 1)))

def reference(features, cotangent, w_stem, w_middle, w_bottom, w_rise, w_final):
    mid_width = w_middle.shape[4]
    top_width = w_bottom.shape[4]
    input_pad = pad_cells(features)
    stem_pre = conv_valid(input_pad, w_stem)
    stem_act = silu_act(stem_pre).astype(jnp.bfloat16)
    half = pool_mean(stem_act)
    half_pad = pad_cells(half)
    mid_pre = conv_valid(half_pad, w_middle)
    mid_act = silu_act(mid_pre).astype(jnp.bfloat16)
    quarter = pool_mean(mid_act)
    quarter_pad = pad_cells(quarter)
    deep_pre = conv_valid(quarter_pad, w_bottom)
    deep_act = silu_act(deep_pre).astype(jnp.bfloat16)
    rise_pad = pad_cells(jnp.concatenate([upsample(deep_act), mid_act], 0))
    rise_pre = conv_valid(rise_pad, w_rise)
    rise_act = silu_act(rise_pre).astype(jnp.bfloat16)
    final_pad = pad_cells(jnp.concatenate([upsample(rise_act), stem_act], 0))
    output = conv_valid(final_pad, w_final).astype(jnp.bfloat16)
    grad_final = weight_grad(final_pad, cotangent)
    final_back = conv_back(pad_cells(cotangent), w_final)
    rise_grad = (pool_sum(final_back[:mid_width]) * silu_slope(rise_pre)).astype(jnp.bfloat16)
    grad_rise = weight_grad(rise_pad, rise_grad)
    rise_back = conv_back(pad_cells(rise_grad), w_rise)
    deep_grad = (pool_sum(rise_back[:top_width]) * silu_slope(deep_pre)).astype(jnp.bfloat16)
    grad_bottom = weight_grad(quarter_pad, deep_grad)
    quarter_back = conv_back(pad_cells(deep_grad), w_bottom)
    mid_grad = ((rise_back[top_width:] + upsample(quarter_back) / 8.0) * silu_slope(mid_pre)).astype(jnp.bfloat16)
    grad_middle = weight_grad(half_pad, mid_grad)
    half_back = conv_back(pad_cells(mid_grad), w_middle)
    stem_grad = ((final_back[mid_width:] + upsample(half_back) / 8.0) * silu_slope(stem_pre)).astype(jnp.bfloat16)
    grad_stem = weight_grad(input_pad, stem_grad)
    cell_count = features.shape[1] * features.shape[2] * features.shape[3]
    fine_scale = 1.0 / math.sqrt(cell_count)
    half_scale = 1.0 / math.sqrt(cell_count / 8.0)
    deep_scale = 1.0 / math.sqrt(cell_count / 64.0)
    return (output, grad_stem * fine_scale, grad_middle * half_scale, grad_bottom * deep_scale, grad_rise * half_scale, grad_final * fine_scale, half_back)
```

```python
import functools
import math

import jax
import jax.numpy as jnp
from jax import lax
from jax.experimental import pallas as pl
from jax.experimental.pallas import tpu as pltpu
from jax.sharding import PartitionSpec as P

BF, F32 = jnp.bfloat16, jnp.float32
AXES = ("grp", "dep", "hgt", "wid")


def mm(a, b):
    return lax.dot_general(a, b, (((1,), (0,)), ((), ())), preferred_element_type=F32)


def mm_nt(a, b):
    return lax.dot_general(a, b, (((1,), (1,)), ((), ())), preferred_element_type=F32)


def mm_split(a, b):
    high = a.astype(BF)
    low = (a - high.astype(F32)).astype(BF)
    return mm(high, b) + mm(low, b)


def silu(v):
    return v * jax.nn.sigmoid(v)


def slope(v):
    g = jax.nn.sigmoid(v)
    return g * (1.0 + v * (1.0 - g))


def pattern(lanes, test):
    row = lax.broadcasted_iota(jnp.int32, (lanes, lanes), 0)
    col = lax.broadcasted_iota(jnp.int32, (lanes, lanes), 1)
    return jnp.where(test(row, col), 1.0, 0.0)


class Halo:
    def __init__(self, index, rows, edges, own, span, sems):
        self.index, self.rows, self.edges, self.own = index, rows, edges, own
        self.w, self.d, self.h = span
        self.send, self.recv = sems

    def fill_edges(self):
        lanes = self.own.shape[1]
        lane = lax.broadcasted_iota(jnp.int32, self.own.shape, 1)
        tile = jnp.zeros(self.own.shape, F32)
        for a in range(self.w):
            for b in range(self.d):
                r = a * self.d + b
                row = self.rows[a + 1, b + 1].astype(F32)
                tile = jnp.where(lane == r, row[:, 0:1], tile)
                tile = jnp.where(lane == lanes // 2 + r, row[:, self.h - 1 : self.h], tile)
        self.own[...] = tile.astype(BF)

    def copies(self, build=True):
        place = {name: lax.axis_index(name) for name in AXES}
        size = {name: lax.axis_size(name) for name in AXES}

        def choices(name):
            i, n = place[name], size[name]
            if n == 1:
                return [(0, 0, True, True)]
            if n == 2:
                return [(0, 0, True, True), (1, 1 - 2 * i, True, True)]
            return [(0, 0, True, True), (1, 1, i < n - 1, i > 0), (2, -1, i > 0, i < n - 1)]

        def cells(step, code, count):
            if code == 0:
                return pl.ds(1, count), pl.ds(1, count)
            up = (1 + step) // 2
            return pl.ds(1 + (count - 1) * up, 1), pl.ds((count + 1) * (1 - up), 1)

        out = []
        for cw, sw, ow, iw in choices("wid"):
            for cd, sd, od, id_ in choices("dep"):
                for ch, sh, oh, ih in choices("hgt"):
                    if cw == 0 and cd == 0 and ch == 0:
                        continue
                    slot = self.index * 27 + (cw * 3 + cd) * 3 + ch
                    target = {"wid": place["wid"] + sw, "dep": place["dep"] + sd, "hgt": place["hgt"] + sh}
                    if not build:
                        out.append((target, [c for c in (ow, od, oh) if c is not True], [c for c in (iw, id_, ih) if c is not True]))
                        continue
                    if ch == 0:
                        from_w, to_w = cells(sw, cw, self.w)
                        from_d, to_d = cells(sd, cd, self.d)
                        source = self.rows.at[from_w, from_d]
                        dest = self.rows.at[to_w, to_d]
                    else:
                        source = self.own
                        dest = self.edges.at[(1 - sh) // 2, 1 - sw, 1 - sd]
                    copy = pltpu.make_async_remote_copy(
                        src_ref=source,
                        dst_ref=dest,
                        send_sem=self.send.at[slot],
                        recv_sem=self.recv.at[slot],
                        device_id=target,
                        device_id_type=pl.DeviceIdType.MESH,
                    )
                    out.append((copy, [c for c in (ow, od, oh) if c is not True], [c for c in (iw, id_, ih) if c is not True]))
        return out

    @staticmethod
    def guarded(conditions, action):
        if not conditions:
            action()
        else:
            pl.when(functools.reduce(jnp.logical_and, conditions))(action)

    def start(self):
        self.fill_edges()
        for copy, can_send, _ in self.copies():
            self.guarded(can_send, copy.start)

    def wait(self):
        for copy, _, can_take in self.copies():
            self.guarded(can_take, copy.wait_recv)

    def finish(self):
        for copy, can_send, _ in self.copies():
            self.guarded(can_send, copy.wait_send)

    def shifted(self, a, b, spread=None, fine=None):
        lanes = self.own.shape[1]
        h = self.h if spread is None else 2 * self.h
        row = self.rows[a, b]
        if spread is not None:
            row = mm(row, spread).astype(BF)
        dw = 0 if a == 0 else 2 if a == self.w + 1 else 1
        dd = 0 if b == 0 else 2 if b == self.d + 1 else 1
        r = (self.w - 1, a - 1, 0)[dw] * self.d + (self.d - 1, b - 1, 0)[dd]
        left = self.edges[0, dw, dd].astype(F32)[:, lanes // 2 + r : lanes // 2 + r + 1]
        right = self.edges[1, dw, dd].astype(F32)[:, r : r + 1]
        lane = lax.broadcasted_iota(jnp.int32, row.shape, 1)
        wide = row.astype(F32)
        before = jnp.where(lane == 0, left, pltpu.roll(wide, 1, 1))
        after = jnp.where(lane == h - 1, right, pltpu.roll(wide, lanes - 1, 1))
        if h < lanes:
            before = jnp.where(lane < h, before, 0.0)
            after = jnp.where(lane < h, after, 0.0)
        return before.astype(BF), row, after.astype(BF)


def step_kernel(cfg, *refs):
    (f0, f1, f2, w, d, h) = cfg
    (feat, cot, w_stem, w_mid, w_bot, w_rise, w_fin, b_mid, b_bot, b_rise, b_fin) = refs[:11]
    (output, grads, half_out) = refs[11:14]
    names = ("feat", "cot", "stem", "half", "mid", "quarter", "deep", "ra", "rg", "dg", "mg")
    refs = refs[14:]
    spans = {0: (w, d, h), 1: (w // 2, d // 2, h // 2), 2: (w // 4, d // 4, h // 4)}
    levels = dict(feat=0, cot=0, stem=0, half=1, mid=1, quarter=2, deep=2, ra=1, rg=1, dg=2, mg=1)
    send, recv = refs[0], refs[1]
    halo = {}
    for i, name in enumerate(names):
        rows, edges, own = refs[2 + 3 * i : 5 + 3 * i]
        halo[name] = Halo(i, rows, edges, own, spans[levels[name]], (send, recv))
    rest = refs[2 + 3 * len(names) :]
    (s_feat, s_cot, s_half, s_quarter, s_rise, s_fin, s_rg, s_dg, s_mg) = rest[:9]
    (stem_pre, mid_pre, deep_pre, rise_pre, fb_pool, fb_skip, rb_skip, stem_grad) = rest[9:]

    for item in halo.values():
        item.rows[...] = jnp.zeros(item.rows.shape, BF)
        item.edges[...] = jnp.zeros(item.edges.shape, BF)
    for a in range(w):
        for b in range(d):
            halo["feat"].rows[a + 1, b + 1] = feat[a, b]
            halo["cot"].rows[a + 1, b + 1] = cot[a, b]

    barrier = pltpu.get_barrier_semaphore()
    for target, can_send, _ in halo["feat"].copies(False):
        Halo.guarded(
            can_send,
            functools.partial(
                pl.semaphore_signal, barrier, 1, device_id=target, device_id_type=pl.DeviceIdType.MESH
            ),
        )
    peers = 1
    for name in ("wid", "dep", "hgt"):
        i, n = lax.axis_index(name), lax.axis_size(name)
        peers = peers * (1 + jnp.minimum(i, 1) + jnp.minimum(n - 1 - i, 1))
    pl.semaphore_wait(barrier, peers - 1)

    lanes = h
    pool = pattern(lanes, lambda r, c: r // 2 == c)
    pool_mean = (pool / 8.0).astype(BF)
    pool_sum = pool.astype(BF)
    spread = pattern(lanes, lambda r, c: c // 2 == r)
    spread_mean = (spread / 8.0).astype(BF)
    spread = spread.astype(BF)

    def stack_shifts(name, target):
        item = halo[name]
        for a in range(item.w + 2):
            for b in range(item.d + 2):
                target[a, b] = jnp.concatenate(item.shifted(a, b), axis=0)

    def stack_pair(coarse, fine, target):
        up, low = halo[coarse], halo[fine]
        for a in range(low.w + 2):
            for b in range(low.d + 2):
                one = up.shifted((a + 1) // 2, (b + 1) // 2, spread)
                two = low.shifted(a, b)
                target[a, b] = jnp.concatenate([v for pair in zip(one, two) for v in pair], axis=0)

    def patch(source, a, b, pair):
        parts = []
        for q in range(pair):
            parts.append(
                jnp.concatenate([source[a + ka, b + kb + q] for ka in range(3) for kb in range(3)], axis=0)
            )
        return parts[0] if pair == 1 else jnp.concatenate(parts, axis=1)

    def over_rows(span, body):
        pair = 2 if span[1] % 2 == 0 else 1
        across = span[1] // pair

        def trip(i, _):
            body(i // across, (i % across) * pair, pair)
            return 0

        count = span[0] * across
        if count == 1:
            body(0, 0, pair)
        else:
            lax.fori_loop(0, count, trip, 0)

    def conv(source, weight, span, store):
        def body(a, b, pair):
            result = mm(weight[...], patch(source, a, b, pair))
            for q in range(pair):
                store(a, b + q, result[:, q * lanes : (q + 1) * lanes])

        over_rows(span, body)

    def wgrad_into(base, patches, grad, width):
        groups = lanes // width
        count = patches.shape[0] // groups
        for g in range(groups):
            pieces = [jnp.zeros_like(grad)] * groups
            pieces[g] = grad
            full = pieces[0] if groups == 1 else jnp.concatenate(pieces, axis=0)
            part = mm_nt(patches[g * count : (g + 1) * count], full)
            grads[base : base + count] += part

    def grad_row(ref, a, b, pair, pad):
        parts = [ref[a + pad, b + pad + q] for q in range(pair)]
        return parts[0] if pair == 1 else jnp.concatenate(parts, axis=1)

    sizes = [27 * f0 * f0, 27 * f0 * f1, 27 * f1 * f2, 27 * (f2 + f1) * f1, 27 * (f1 + f0) * f0]
    bases = [sum(sizes[:i]) // lanes for i in range(5)]
    grads[...] = jnp.zeros(grads.shape, F32)

    halo["feat"].start()
    halo["cot"].start()
    halo["feat"].wait()
    stack_shifts("feat", s_feat)

    def stem_store(a, b, value):
        stem_pre[a, b] = value
        halo["stem"].rows[a + 1, b + 1] = silu(value).astype(BF)

    conv(s_feat, w_stem, spans[0], stem_store)

    def pooled(fine, coarse):
        low, up = halo[fine], halo[coarse]
        for a in range(up.w):
            for b in range(up.d):
                cat = [low.rows[2 * a + 1 + i, 2 * b + 1 + j] for i in range(2) for j in range(2)]
                total = mm(cat[0], pool_mean) + mm(cat[1], pool_mean) + mm(cat[2], pool_mean) + mm(cat[3], pool_mean)
                up.rows[a + 1, b + 1] = total.astype(BF)

    pooled("stem", "half")
    halo["half"].start()
    halo["stem"].start()
    halo["cot"].wait()
    stack_shifts("cot", s_cot)
    fb_pool[...] = jnp.zeros(fb_pool.shape, F32)

    def back_store(a, b, value):
        fb_pool[a // 2, b // 2] += value[:f1]
        fb_skip[a, b] = value[f1:]

    conv(s_cot, b_fin, spans[0], back_store)
    halo["half"].wait()
    stack_shifts("half", s_half)

    def mid_store(a, b, value):
        mid_pre[a, b] = value
        halo["mid"].rows[a + 1, b + 1] = silu(value).astype(BF)

    conv(s_half, w_mid, spans[1], mid_store)
    pooled("mid", "quarter")
    halo["quarter"].start()
    halo["mid"].start()
    halo["quarter"].wait()
    stack_shifts("quarter", s_quarter)

    def deep_store(a, b, value):
        deep_pre[a, b] = value
        halo["deep"].rows[a + 1, b + 1] = silu(value).astype(BF)

    conv(s_quarter, w_bot, spans[2], deep_store)
    halo["deep"].start()
    halo["mid"].wait()
    halo["deep"].wait()
    stack_pair("deep", "mid", s_rise)

    def rise_store(a, b, value):
        rise_pre[a, b] = value
        halo["ra"].rows[a + 1, b + 1] = silu(value).astype(BF)
        grad = mm_split(fb_pool[a, b], pool_sum) * slope(value)
        halo["rg"].rows[a + 1, b + 1] = grad.astype(BF)

    conv(s_rise, w_rise, spans[1], rise_store)
    halo["rg"].start()
    halo["ra"].start()
    halo["rg"].wait()
    stack_shifts("rg", s_rg)
    deep_sum = [[None] * spans[2][1] for _ in range(spans[2][0])]

    pair1 = 2 if spans[1][1] % 2 == 0 else 1
    for a in range(spans[1][0]):
        for b in range(0, spans[1][1], pair1):
            result = mm(b_rise[...], patch(s_rg, a, b, pair1))
            for q in range(pair1):
                value = result[:, q * lanes : (q + 1) * lanes]
                rb_skip[a, b + q] = value[f2:]
                at, bt = a // 2, (b + q) // 2
                old = deep_sum[at][bt]
                deep_sum[at][bt] = value[:f2] if old is None else old + value[:f2]
    for a in range(spans[2][0]):
        for b in range(spans[2][1]):
            grad = mm_split(deep_sum[a][b], pool_sum) * slope(deep_pre[a, b])
            halo["dg"].rows[a + 1, b + 1] = grad.astype(BF)
    halo["dg"].start()

    def rise_wgrad(a, b, pair):
        wgrad_into(bases[3], patch(s_rise, a, b, pair), grad_row(halo["rg"].rows, a, b, pair, 1), f1)

    over_rows(spans[1], rise_wgrad)
    halo["dg"].wait()
    stack_shifts("dg", s_dg)

    def quarter_store(a, b, value):
        wide = mm_split(value, spread_mean)
        for i in range(2):
            for j in range(2):
                at, bt = 2 * a + i, 2 * b + j
                grad = (rb_skip[at, bt] + wide) * slope(mid_pre[at, bt])
                halo["mg"].rows[at + 1, bt + 1] = grad.astype(BF)

    conv(s_dg, b_bot, spans[2], quarter_store)
    halo["mg"].start()

    def bottom_wgrad(a, b, pair):
        wgrad_into(bases[2], patch(s_quarter, a, b, pair), grad_row(halo["dg"].rows, a, b, pair, 1), f2)

    over_rows(spans[2], bottom_wgrad)

    def mid_wgrad(a, b, pair):
        wgrad_into(bases[1], patch(s_half, a, b, pair), grad_row(halo["mg"].rows, a, b, pair, 1), f1)

    over_rows(spans[1], mid_wgrad)

    halo["stem"].wait()
    halo["ra"].wait()
    stack_pair("ra", "stem", s_fin)

    def final(a, b, pair):
        cells = patch(s_fin, a, b, pair)
        result = mm(w_fin[...], cells)
        for q in range(pair):
            output[a, b + q] = result[:, q * lanes : (q + 1) * lanes].astype(BF)
        wgrad_into(bases[4], cells, grad_row(cot, a, b, pair, 0), f0)

    over_rows(spans[0], final)

    halo["mg"].wait()
    stack_shifts("mg", s_mg)

    def half_store(a, b, value):
        half_out[a, b] = value
        wide = mm_split(value, spread_mean)
        for i in range(2):
            for j in range(2):
                at, bt = 2 * a + i, 2 * b + j
                grad = (fb_skip[at, bt] + wide) * slope(stem_pre[at, bt])
                stem_grad[at, bt] = grad.astype(BF)

    conv(s_mg, b_mid, spans[1], half_store)

    def stem_wgrad(a, b, pair):
        wgrad_into(bases[0], patch(s_feat, a, b, pair), grad_row(stem_grad, a, b, pair, 0), f0)

    over_rows(spans[0], stem_wgrad)
    for item in halo.values():
        item.finish()


def local(features, cotangent, w_stem, w_middle, w_bottom, w_rise, w_final):
    f0, w, d, h = features.shape
    f1, f2 = w_middle.shape[4], w_bottom.shape[4]
    spans = {0: (w, d), 1: (w // 2, d // 2), 2: (w // 4, d // 4)}
    halos = [(f0, 0), (f0, 0), (f0, 0), (f0, 1), (f1, 1), (f1, 2), (f2, 2), (f1, 1), (f1, 1), (f2, 2), (f1, 1)]
    scratch = [pltpu.SemaphoreType.DMA((27 * len(halos),)), pltpu.SemaphoreType.DMA((27 * len(halos),))]
    for c, level in halos:
        a, b = spans[level]
        scratch += [
            pltpu.VMEM((a + 2, b + 2, c, h), BF),
            pltpu.VMEM((2, 3, 3, c, h), BF),
            pltpu.VMEM((c, h), BF),
        ]
    for c, level in [(f0, 0), (f0, 0), (f0, 1), (f1, 2), (f2 + f1, 1), (f1 + f0, 0), (f1, 1), (f2, 2), (f1, 1)]:
        a, b = spans[level]
        scratch.append(pltpu.VMEM((a + 2, b + 2, 3 * c, h), BF))
    for c, level in [(f0, 0), (f1, 1), (f2, 2), (f1, 1), (f1, 1), (f0, 0), (f1, 1)]:
        scratch.append(pltpu.VMEM((*spans[level], c, h), F32))
    scratch.append(pltpu.VMEM((w, d, f0, h), BF))

    def forward(v):
        return v.reshape(-1, v.shape[4]).T

    def backward(v):
        return v[::-1, ::-1, ::-1].reshape(27, v.shape[3], v.shape[4]).transpose(1, 0, 2).reshape(v.shape[3], -1)

    weights = (w_stem, w_middle, w_bottom, w_rise, w_final)
    total = sum(v.size for v in weights) // h
    vmem = pl.BlockSpec(memory_space=pltpu.VMEM)
    out, grads, half_back = pl.pallas_call(
        functools.partial(step_kernel, (f0, f1, f2, w, d, h)),
        out_shape=(
            jax.ShapeDtypeStruct((w, d, f0, h), BF),
            jax.ShapeDtypeStruct((total, h), F32),
            jax.ShapeDtypeStruct((w // 2, d // 2, f0, h), F32),
        ),
        in_specs=[vmem] * 11,
        out_specs=(vmem,) * 3,
        scratch_shapes=scratch,
        compiler_params=pltpu.CompilerParams(
            collective_id=0, has_side_effects=True, vmem_limit_bytes=60 << 20
        ),
        name="unet_step",
    )(
        features.transpose(1, 2, 0, 3),
        cotangent.transpose(1, 2, 0, 3),
        *[forward(v) for v in weights],
        *[backward(v) for v in weights[1:]],
    )
    summed = reduce_all(grads.astype(BF))
    cells = w * d * h * lax.axis_size("dep") * lax.axis_size("hgt") * lax.axis_size("wid")
    fine, mid, deep = (1.0 / math.sqrt(cells / k) for k in (1.0, 8.0, 64.0))
    results, base = [], 0
    for v, scale in zip(weights, (fine, mid, deep, mid, fine)):
        rows, width = v.size // h, v.shape[4]
        part = summed[base : base + rows].astype(F32) * scale
        base += rows
        part = part.reshape(rows, h // width, width).transpose(1, 0, 2).reshape(v.shape)
        results.append(part)
    return (out.transpose(2, 0, 1, 3), *results, half_back[..., : h // 2].transpose(2, 0, 1, 3))


def reduce_all(grads):
    return lax.psum(grads, ("dep", "hgt", "wid"))


def solution(mesh):
    placed = (P("grp", "wid", "dep", "hgt"), P("grp", "wid", "dep", "hgt"), P(), P(), P(), P(), P())
    grad = P("grp", None, None, None, None)
    return jax.shard_map(
        local,
        mesh=mesh,
        in_specs=placed,
        out_specs=(P("grp", "wid", "dep", "hgt"), grad, grad, grad, grad, grad, P("grp", "wid", "dep", "hgt")),
        check_vma=False,
    )
```

```python
import functools
import math

import jax
import jax.numpy as jnp
from jax import lax
from jax.experimental import pallas as pl
from jax.experimental.pallas import tpu as pltpu
from jax.sharding import PartitionSpec as P

BF, F32 = jnp.bfloat16, jnp.float32
SEGMENTS = ((3, 4), (2, 1), (0,))
AXES = ("grp", "dep", "hgt", "wid")


def mm(a, b):
    return lax.dot_general(a, b, (((1,), (0,)), ((), ())), preferred_element_type=F32)


def mm_nt(a, b):
    return lax.dot_general(a, b, (((1,), (1,)), ((), ())), preferred_element_type=F32)


def mm_split(a, b):
    high = a.astype(BF)
    low = (a - high.astype(F32)).astype(BF)
    return mm(high, b) + mm(low, b)


def silu(v):
    return v * jax.nn.sigmoid(v)


def slope(v):
    g = jax.nn.sigmoid(v)
    return g * (1.0 + v * (1.0 - g))


def pattern(lanes, test):
    row = lax.broadcasted_iota(jnp.int32, (lanes, lanes), 0)
    col = lax.broadcasted_iota(jnp.int32, (lanes, lanes), 1)
    return jnp.where(test(row, col), 1.0, 0.0)


class Halo:
    def __init__(self, index, rows, edges, own, span, sems):
        self.index, self.rows, self.edges, self.own = index, rows, edges, own
        self.w, self.d, self.h = span
        self.send, self.recv = sems

    def fill_edges(self):
        lanes = self.own.shape[1]
        lane = lax.broadcasted_iota(jnp.int32, self.own.shape, 1)
        tile = jnp.zeros(self.own.shape, F32)
        for a in range(self.w):
            for b in range(self.d):
                r = a * self.d + b
                row = self.rows[a + 1, b + 1].astype(F32)
                tile = jnp.where(lane == r, row[:, 0:1], tile)
                tile = jnp.where(lane == lanes // 2 + r, row[:, self.h - 1 : self.h], tile)
        self.own[...] = tile.astype(BF)

    def copies(self, build=True):
        place = {name: lax.axis_index(name) for name in AXES}
        size = {name: lax.axis_size(name) for name in AXES}

        def choices(name):
            i, n = place[name], size[name]
            if n == 1:
                return [(0, 0, True, True)]
            if n == 2:
                return [(0, 0, True, True), (1, 1 - 2 * i, True, True)]
            return [(0, 0, True, True), (1, 1, i < n - 1, i > 0), (2, -1, i > 0, i < n - 1)]

        def cells(step, code, count):
            if code == 0:
                return pl.ds(1, count), pl.ds(1, count)
            up = (1 + step) // 2
            return pl.ds(1 + (count - 1) * up, 1), pl.ds((count + 1) * (1 - up), 1)

        out = []
        for cw, sw, ow, iw in choices("wid"):
            for cd, sd, od, id_ in choices("dep"):
                for ch, sh, oh, ih in choices("hgt"):
                    if cw == 0 and cd == 0 and ch == 0:
                        continue
                    slot = self.index * 27 + (cw * 3 + cd) * 3 + ch
                    target = {"wid": place["wid"] + sw, "dep": place["dep"] + sd, "hgt": place["hgt"] + sh}
                    if not build:
                        out.append((target, [c for c in (ow, od, oh) if c is not True], [c for c in (iw, id_, ih) if c is not True]))
                        continue
                    if ch == 0:
                        from_w, to_w = cells(sw, cw, self.w)
                        from_d, to_d = cells(sd, cd, self.d)
                        source = self.rows.at[from_w, from_d]
                        dest = self.rows.at[to_w, to_d]
                    else:
                        source = self.own
                        dest = self.edges.at[(1 - sh) // 2, 1 - sw, 1 - sd]
                    copy = pltpu.make_async_remote_copy(
                        src_ref=source,
                        dst_ref=dest,
                        send_sem=self.send.at[slot],
                        recv_sem=self.recv.at[slot],
                        device_id=target,
                        device_id_type=pl.DeviceIdType.MESH,
                    )
                    out.append((copy, [c for c in (ow, od, oh) if c is not True], [c for c in (iw, id_, ih) if c is not True]))
        return out

    @staticmethod
    def guarded(conditions, action):
        if not conditions:
            action()
        else:
            pl.when(functools.reduce(jnp.logical_and, conditions))(action)

    def start(self):
        self.fill_edges()
        for copy, can_send, _ in self.copies():
            self.guarded(can_send, copy.start)

    def wait(self):
        for copy, _, can_take in self.copies():
            self.guarded(can_take, copy.wait_recv)

    def finish(self):
        for copy, can_send, _ in self.copies():
            self.guarded(can_send, copy.wait_send)

    def shifted(self, a, b, spread=None, fine=None):
        lanes = self.own.shape[1]
        h = self.h if spread is None else 2 * self.h
        row = self.rows[a, b]
        if spread is not None:
            row = mm(row, spread).astype(BF)
        dw = 0 if a == 0 else 2 if a == self.w + 1 else 1
        dd = 0 if b == 0 else 2 if b == self.d + 1 else 1
        r = (self.w - 1, a - 1, 0)[dw] * self.d + (self.d - 1, b - 1, 0)[dd]
        left = self.edges[0, dw, dd].astype(F32)[:, lanes // 2 + r : lanes // 2 + r + 1]
        right = self.edges[1, dw, dd].astype(F32)[:, r : r + 1]
        lane = lax.broadcasted_iota(jnp.int32, row.shape, 1)
        wide = row.astype(F32)
        before = jnp.where(lane == 0, left, pltpu.roll(wide, 1, 1))
        after = jnp.where(lane == h - 1, right, pltpu.roll(wide, lanes - 1, 1))
        if h < lanes:
            before = jnp.where(lane < h, before, 0.0)
            after = jnp.where(lane < h, after, 0.0)
        return before.astype(BF), row, after.astype(BF)


def at(name, position):
    return {n: position if n == name else lax.axis_index(n) for n in ("dep", "hgt", "wid")}


class Summed:
    order = ("wid", "hgt", "dep")

    def __init__(self, full, buffers, send, recv):
        self.total = buffers[0]
        self.levels = [(buffers[0], buffers[1], buffers[2]), buffers[3:6], buffers[6:9]]
        self.full, self.send, self.recv = full, send, recv
        self.stage, self.open, self.sent = 0, [], []

    def exchange(self, stage, name, pieces):
        i, n = lax.axis_index(name), lax.axis_size(name)
        self.open = []
        for k in range(1, n):
            source, dest = pieces(lax.rem(i + k, n), i)
            copy = pltpu.make_async_remote_copy(
                src_ref=source,
                dst_ref=dest,
                send_sem=self.send.at[stage, k],
                recv_sem=self.recv.at[stage, k],
                device_id=at(name, lax.rem(i + k, n)),
                device_id_type=pl.DeviceIdType.MESH,
            )
            copy.start()
            self.open.append(copy)
            self.sent.append(copy)

    def arrive(self):
        for copy in self.open:
            copy.wait_recv()
        self.open = []

    def step(self):
        stage = self.stage
        self.stage += 1
        if stage > 0:
            self.arrive()
        if 0 < stage <= 3:
            name = self.order[stage - 1]
            i, n = lax.axis_index(name), lax.axis_size(name)
            held, _, came = self.levels[stage - 1]
            m = held.shape[0] // n
            value = held[part(i, m)]
            for k in range(1, n):
                value = value + came[part(lax.rem(i + k, n), m)].astype(F32)
            if stage < 3:
                self.levels[stage][0][...] = value
            else:
                place = 0
                for axis in self.order:
                    place = place * lax.axis_size(axis) + lax.axis_index(axis)
                self.full[part(place, m)] = value.astype(BF)
        if stage < 3:
            held, wire, came = self.levels[stage]
            m = held.shape[0] // lax.axis_size(self.order[stage])
            wire[...] = held[...].astype(BF)
            self.exchange(stage, self.order[stage], lambda to, me: (wire.at[part(to, m)], came.at[part(me, m)]))
        elif stage < 6:
            depth = 6 - stage
            place, count = 0, 1
            for axis in self.order[:depth]:
                place = place * lax.axis_size(axis) + lax.axis_index(axis)
                count *= lax.axis_size(axis)
            m = self.full.shape[0] // count
            piece = self.full.at[part(place, m)]
            self.exchange(stage, self.order[depth - 1], lambda to, me: (piece, piece))

    def finish(self):
        while self.stage < 7:
            self.step()
        for copy in self.sent:
            copy.wait_send()


def part(i, m):
    return pl.ds(pl.multiple_of(i * m, 16), m)


def step_kernel(cfg, *refs):
    (f0, f1, f2, w, d, h) = cfg
    (feat, cot, w_stem, w_mid, w_bot, w_rise, w_fin, b_mid, b_bot, b_rise, b_fin) = refs[:11]
    (output, full0, full1, full2, half_out) = refs[11:16]
    names = ("feat", "cot", "stem", "half", "mid", "quarter", "deep", "ra", "rg", "dg", "mg")
    refs = refs[16:]
    spans = {0: (w, d, h), 1: (w // 2, d // 2, h // 2), 2: (w // 4, d // 4, h // 4)}
    levels = dict(feat=0, cot=0, stem=0, half=1, mid=1, quarter=2, deep=2, ra=1, rg=1, dg=2, mg=1)
    send, recv = refs[0], refs[1]
    halo = {}
    for i, name in enumerate(names):
        rows, edges, own = refs[2 + 3 * i : 5 + 3 * i]
        halo[name] = Halo(i, rows, edges, own, spans[levels[name]], (send, recv))
    rest = refs[2 + 3 * len(names) :]
    (s_feat, s_cot, s_half, s_quarter, s_rise, s_fin, s_rg, s_dg, s_mg) = rest[:9]
    (stem_pre, mid_pre, deep_pre, rise_pre, fb_pool, fb_skip, rb_skip, stem_grad) = rest[9:17]
    rest = rest[17:]
    sums = [
        Summed(full, rest[11 * i : 11 * i + 9], rest[11 * i + 9], rest[11 * i + 10])
        for i, full in enumerate((full0, full1, full2))
    ]

    for item in halo.values():
        item.rows[...] = jnp.zeros(item.rows.shape, BF)
        item.edges[...] = jnp.zeros(item.edges.shape, BF)
    for a in range(w):
        for b in range(d):
            halo["feat"].rows[a + 1, b + 1] = feat[a, b]
            halo["cot"].rows[a + 1, b + 1] = cot[a, b]

    barrier = pltpu.get_barrier_semaphore()
    for target, can_send, _ in halo["feat"].copies(False):
        Halo.guarded(
            can_send,
            functools.partial(
                pl.semaphore_signal, barrier, 1, device_id=target, device_id_type=pl.DeviceIdType.MESH
            ),
        )
    others = 0
    for name in ("dep", "hgt"):
        i, n = lax.axis_index(name), lax.axis_size(name)
        for k in range(1, n):
            other = lax.rem(i + k, n)
            far = jnp.logical_or(other - i > 1, i - other > 1)
            if n > 2:
                Halo.guarded(
                    [far],
                    functools.partial(
                        pl.semaphore_signal, barrier, 1, device_id=at(name, other), device_id_type=pl.DeviceIdType.MESH
                    ),
                )
        others = others + n - (1 + jnp.minimum(i, 1) + jnp.minimum(n - 1 - i, 1))
    peers = 1
    for name in ("wid", "dep", "hgt"):
        i, n = lax.axis_index(name), lax.axis_size(name)
        peers = peers * (1 + jnp.minimum(i, 1) + jnp.minimum(n - 1 - i, 1))
    pl.semaphore_wait(barrier, peers - 1 + others)

    lanes = h
    pool = pattern(lanes, lambda r, c: r // 2 == c)
    pool_mean = (pool / 8.0).astype(BF)
    pool_sum = pool.astype(BF)
    spread = pattern(lanes, lambda r, c: c // 2 == r)
    spread_mean = (spread / 8.0).astype(BF)
    spread = spread.astype(BF)

    def stack_shifts(name, target):
        item = halo[name]
        for a in range(item.w + 2):
            for b in range(item.d + 2):
                target[a, b] = jnp.concatenate(item.shifted(a, b), axis=0)

    def stack_pair(coarse, fine, target):
        up, low = halo[coarse], halo[fine]
        for a in range(low.w + 2):
            for b in range(low.d + 2):
                one = up.shifted((a + 1) // 2, (b + 1) // 2, spread)
                two = low.shifted(a, b)
                target[a, b] = jnp.concatenate([v for pair in zip(one, two) for v in pair], axis=0)

    def patch(source, a, b, pair):
        parts = []
        for q in range(pair):
            parts.append(
                jnp.concatenate([source[a + ka, b + kb + q] for ka in range(3) for kb in range(3)], axis=0)
            )
        return parts[0] if pair == 1 else jnp.concatenate(parts, axis=1)

    def over_rows(span, body):
        pair = 2 if span[1] % 2 == 0 else 1
        across = span[1] // pair

        def trip(i, _):
            body(i // across, (i % across) * pair, pair)
            return 0

        count = span[0] * across
        if count == 1:
            body(0, 0, pair)
        else:
            lax.fori_loop(0, count, trip, 0)

    def conv(source, weight, span, store):
        def body(a, b, pair):
            result = mm(weight[...], patch(source, a, b, pair))
            for q in range(pair):
                store(a, b + q, result[:, q * lanes : (q + 1) * lanes])

        over_rows(span, body)

    def wgrad_into(base, patches, grad, width):
        groups = lanes // width
        count = patches.shape[0] // groups
        for g in range(groups):
            pieces = [jnp.zeros_like(grad)] * groups
            pieces[g] = grad
            full = pieces[0] if groups == 1 else jnp.concatenate(pieces, axis=0)
            value = mm_nt(patches[g * count : (g + 1) * count], full)
            where = sums[base[0]].total
            where[base[1] : base[1] + count] += value

    def grad_row(ref, a, b, pair, pad):
        parts = [ref[a + pad, b + pad + q] for q in range(pair)]
        return parts[0] if pair == 1 else jnp.concatenate(parts, axis=1)

    sizes = [27 * f0 * f0, 27 * f0 * f1, 27 * f1 * f2, 27 * (f2 + f1) * f1, 27 * (f1 + f0) * f0]
    rows_of = [v // lanes for v in sizes]
    bases = {i: (seg, sum(rows_of[j] for j in SEGMENTS[seg][: SEGMENTS[seg].index(i)])) for seg in range(3) for i in SEGMENTS[seg]}
    for item in sums:
        item.total[...] = jnp.zeros(item.total.shape, F32)

    halo["feat"].start()
    halo["cot"].start()
    halo["feat"].wait()
    stack_shifts("feat", s_feat)

    def stem_store(a, b, value):
        stem_pre[a, b] = value
        halo["stem"].rows[a + 1, b + 1] = silu(value).astype(BF)

    conv(s_feat, w_stem, spans[0], stem_store)

    def pooled(fine, coarse):
        low, up = halo[fine], halo[coarse]
        for a in range(up.w):
            for b in range(up.d):
                cat = [low.rows[2 * a + 1 + i, 2 * b + 1 + j] for i in range(2) for j in range(2)]
                total = mm(cat[0], pool_mean) + mm(cat[1], pool_mean) + mm(cat[2], pool_mean) + mm(cat[3], pool_mean)
                up.rows[a + 1, b + 1] = total.astype(BF)

    pooled("stem", "half")
    halo["half"].start()
    halo["stem"].start()
    halo["cot"].wait()
    stack_shifts("cot", s_cot)
    fb_pool[...] = jnp.zeros(fb_pool.shape, F32)

    def back_store(a, b, value):
        fb_pool[a // 2, b // 2] += value[:f1]
        fb_skip[a, b] = value[f1:]

    conv(s_cot, b_fin, spans[0], back_store)
    halo["half"].wait()
    stack_shifts("half", s_half)

    def mid_store(a, b, value):
        mid_pre[a, b] = value
        halo["mid"].rows[a + 1, b + 1] = silu(value).astype(BF)

    conv(s_half, w_mid, spans[1], mid_store)
    pooled("mid", "quarter")
    halo["quarter"].start()
    halo["mid"].start()
    halo["quarter"].wait()
    stack_shifts("quarter", s_quarter)

    def deep_store(a, b, value):
        deep_pre[a, b] = value
        halo["deep"].rows[a + 1, b + 1] = silu(value).astype(BF)

    conv(s_quarter, w_bot, spans[2], deep_store)
    halo["deep"].start()
    halo["mid"].wait()
    halo["deep"].wait()
    stack_pair("deep", "mid", s_rise)

    def rise_store(a, b, value):
        rise_pre[a, b] = value
        halo["ra"].rows[a + 1, b + 1] = silu(value).astype(BF)
        grad = mm_split(fb_pool[a, b], pool_sum) * slope(value)
        halo["rg"].rows[a + 1, b + 1] = grad.astype(BF)

    conv(s_rise, w_rise, spans[1], rise_store)
    halo["rg"].start()
    halo["ra"].start()
    halo["rg"].wait()
    stack_shifts("rg", s_rg)
    deep_sum = [[None] * spans[2][1] for _ in range(spans[2][0])]

    pair1 = 2 if spans[1][1] % 2 == 0 else 1
    for a in range(spans[1][0]):
        for b in range(0, spans[1][1], pair1):
            result = mm(b_rise[...], patch(s_rg, a, b, pair1))
            for q in range(pair1):
                value = result[:, q * lanes : (q + 1) * lanes]
                rb_skip[a, b + q] = value[f2:]
                ap, bt = a // 2, (b + q) // 2
                old = deep_sum[ap][bt]
                deep_sum[ap][bt] = value[:f2] if old is None else old + value[:f2]
    for a in range(spans[2][0]):
        for b in range(spans[2][1]):
            grad = mm_split(deep_sum[a][b], pool_sum) * slope(deep_pre[a, b])
            halo["dg"].rows[a + 1, b + 1] = grad.astype(BF)
    halo["dg"].start()

    def rise_wgrad(a, b, pair):
        wgrad_into(bases[3], patch(s_rise, a, b, pair), grad_row(halo["rg"].rows, a, b, pair, 1), f1)

    over_rows(spans[1], rise_wgrad)
    halo["stem"].wait()
    halo["ra"].wait()
    stack_pair("ra", "stem", s_fin)

    def final(a, b, pair):
        cells = patch(s_fin, a, b, pair)
        result = mm(w_fin[...], cells)
        for q in range(pair):
            output[a, b + q] = result[:, q * lanes : (q + 1) * lanes].astype(BF)
        wgrad_into(bases[4], cells, grad_row(cot, a, b, pair, 0), f0)

    over_rows(spans[0], final)
    sums[0].step()
    halo["dg"].wait()
    stack_shifts("dg", s_dg)

    def quarter_store(a, b, value):
        wide = mm_split(value, spread_mean)
        for i in range(2):
            for j in range(2):
                at_, bt = 2 * a + i, 2 * b + j
                grad = (rb_skip[at_, bt] + wide) * slope(mid_pre[at_, bt])
                halo["mg"].rows[at_ + 1, bt + 1] = grad.astype(BF)

    conv(s_dg, b_bot, spans[2], quarter_store)
    halo["mg"].start()
    sums[0].step()

    def bottom_wgrad(a, b, pair):
        wgrad_into(bases[2], patch(s_quarter, a, b, pair), grad_row(halo["dg"].rows, a, b, pair, 1), f2)

    over_rows(spans[2], bottom_wgrad)

    def mid_wgrad(a, b, pair):
        wgrad_into(bases[1], patch(s_half, a, b, pair), grad_row(halo["mg"].rows, a, b, pair, 1), f1)

    over_rows(spans[1], mid_wgrad)
    sums[1].step()
    halo["mg"].wait()
    stack_shifts("mg", s_mg)

    def half_store(a, b, value):
        half_out[a, b] = value
        wide = mm_split(value, spread_mean)
        for i in range(2):
            for j in range(2):
                at_, bt = 2 * a + i, 2 * b + j
                grad = (fb_skip[at_, bt] + wide) * slope(stem_pre[at_, bt])
                stem_grad[at_, bt] = grad.astype(BF)

    conv(s_mg, b_mid, spans[1], half_store)
    sums[0].step()
    sums[1].step()

    def stem_wgrad(a, b, pair):
        wgrad_into(bases[0], patch(s_feat, a, b, pair), grad_row(stem_grad, a, b, pair, 0), f0)

    over_rows(spans[0], stem_wgrad)
    sums[2].step()
    sums[0].step()
    sums[1].step()
    for _ in range(3):
        for item in (sums[2], sums[0], sums[1]):
            item.step()
    for item in (sums[2], sums[0], sums[1]):
        item.finish()
    for item in halo.values():
        item.finish()


def local(features, cotangent, w_stem, w_middle, w_bottom, w_rise, w_final):
    f0, w, d, h = features.shape
    f1, f2 = w_middle.shape[4], w_bottom.shape[4]
    spans = {0: (w, d), 1: (w // 2, d // 2), 2: (w // 4, d // 4)}
    halos = [(f0, 0), (f0, 0), (f0, 0), (f0, 1), (f1, 1), (f1, 2), (f2, 2), (f1, 1), (f1, 1), (f2, 2), (f1, 1)]
    scratch = [pltpu.SemaphoreType.DMA((27 * len(halos),)), pltpu.SemaphoreType.DMA((27 * len(halos),))]
    for c, level in halos:
        a, b = spans[level]
        scratch += [
            pltpu.VMEM((a + 2, b + 2, c, h), BF),
            pltpu.VMEM((2, 3, 3, c, h), BF),
            pltpu.VMEM((c, h), BF),
        ]
    for c, level in [(f0, 0), (f0, 0), (f0, 1), (f1, 2), (f2 + f1, 1), (f1 + f0, 0), (f1, 1), (f2, 2), (f1, 1)]:
        a, b = spans[level]
        scratch.append(pltpu.VMEM((a + 2, b + 2, 3 * c, h), BF))
    for c, level in [(f0, 0), (f1, 1), (f2, 2), (f1, 1), (f1, 1), (f0, 0), (f1, 1)]:
        scratch.append(pltpu.VMEM((*spans[level], c, h), F32))
    scratch.append(pltpu.VMEM((w, d, f0, h), BF))
    weights = (w_stem, w_middle, w_bottom, w_rise, w_final)
    counts = [lax.axis_size(axis) for axis in Summed.order]
    unit = 16 * math.prod(counts)
    lengths = []
    for members in SEGMENTS:
        rows = -(-sum(weights[i].size // h for i in members) // unit) * unit
        lengths.append(rows)
        for n in counts:
            scratch += [pltpu.VMEM((rows, h), F32), pltpu.VMEM((rows, h), BF), pltpu.VMEM((rows, h), BF)]
            rows //= n
        scratch += [pltpu.SemaphoreType.DMA((6, max(counts))), pltpu.SemaphoreType.DMA((6, max(counts)))]

    def forward(v):
        return v.reshape(-1, v.shape[4]).T

    def backward(v):
        return v[::-1, ::-1, ::-1].reshape(27, v.shape[3], v.shape[4]).transpose(1, 0, 2).reshape(v.shape[3], -1)

    vmem = pl.BlockSpec(memory_space=pltpu.VMEM)
    out, *packed, half_back = pl.pallas_call(
        functools.partial(step_kernel, (f0, f1, f2, w, d, h)),
        out_shape=(
            jax.ShapeDtypeStruct((w, d, f0, h), BF),
            *[jax.ShapeDtypeStruct((rows, h), BF) for rows in lengths],
            jax.ShapeDtypeStruct((w // 2, d // 2, f0, h), F32),
        ),
        in_specs=[vmem] * 11,
        out_specs=(vmem,) * 5,
        scratch_shapes=scratch,
        compiler_params=pltpu.CompilerParams(
            collective_id=0, has_side_effects=True, vmem_limit_bytes=60 << 20
        ),
        name="unet_step",
    )(
        features.transpose(1, 2, 0, 3),
        cotangent.transpose(1, 2, 0, 3),
        *[forward(v) for v in weights],
        *[backward(v) for v in weights[1:]],
    )
    cells = w * d * h * lax.axis_size("dep") * lax.axis_size("hgt") * lax.axis_size("wid")
    fine, mid, deep = (1.0 / math.sqrt(cells / k) for k in (1.0, 8.0, 64.0))
    scales = (fine, mid, deep, mid, fine)

    def unpack(*refs):
        for members, source in zip(SEGMENTS, refs[:3]):
            base = 0
            for i in members:
                target = refs[3 + i]
                width = target.shape[1]
                rows = target.shape[0] * width // h
                value = source[base : base + rows].astype(F32) * scales[i]
                base += rows
                for g in range(h // width):
                    target[g * rows : (g + 1) * rows] = value[:, g * width : (g + 1) * width]

    flat = pl.pallas_call(
        unpack,
        out_shape=tuple(jax.ShapeDtypeStruct((v.size // v.shape[4], v.shape[4]), F32) for v in weights),
        in_specs=[vmem] * 3,
        out_specs=(vmem,) * 5,
        compiler_params=pltpu.CompilerParams(vmem_limit_bytes=32 << 20),
        name="unpack",
    )(*packed)
    results = [r.reshape(v.shape) for r, v in zip(flat, weights)]
    return (out.transpose(2, 0, 1, 3), *results, half_back[..., : h // 2].transpose(2, 0, 1, 3))


def solution(mesh):
    placed = (P("grp", "wid", "dep", "hgt"), P("grp", "wid", "dep", "hgt"), P(), P(), P(), P(), P())
    grad = P("grp", None, None, None, None)
    return jax.shard_map(
        local,
        mesh=mesh,
        in_specs=placed,
        out_specs=(P("grp", "wid", "dep", "hgt"), grad, grad, grad, grad, grad, P("grp", "wid", "dep", "hgt")),
        check_vma=False,
    )
```

```python
import functools
import math

import jax
import jax.numpy as jnp
from jax import lax
from jax.experimental import pallas as pl
from jax.experimental.pallas import tpu as pltpu
from jax.sharding import PartitionSpec as P

BF, F32 = jnp.bfloat16, jnp.float32
SEGMENTS = ((3,), (2, 4), (1, 0))
AXES = ("grp", "dep", "hgt", "wid")


def mm(a, b):
    return lax.dot_general(a, b, (((1,), (0,)), ((), ())), preferred_element_type=F32)


def mm_nt(a, b):
    return lax.dot_general(a, b, (((1,), (1,)), ((), ())), preferred_element_type=F32)


def mm_split(a, b):
    high = a.astype(BF)
    low = (a - high.astype(F32)).astype(BF)
    return mm(high, b) + mm(low, b)


def silu(v):
    return v * jax.nn.sigmoid(v)


def slope(v):
    g = jax.nn.sigmoid(v)
    return g * (1.0 + v * (1.0 - g))


def pattern(lanes, test):
    row = lax.broadcasted_iota(jnp.int32, (lanes, lanes), 0)
    col = lax.broadcasted_iota(jnp.int32, (lanes, lanes), 1)
    return jnp.where(test(row, col), 1.0, 0.0)


class Halo:
    def __init__(self, index, rows, edges, own, span, sems):
        self.index, self.rows, self.edges, self.own = index, rows, edges, own
        self.w, self.d, self.h = span
        self.send, self.recv = sems

    def fill_edges(self):
        lanes = self.own.shape[1]
        lane = lax.broadcasted_iota(jnp.int32, self.own.shape, 1)
        tile = jnp.zeros(self.own.shape, F32)
        for a in range(self.w):
            for b in range(self.d):
                r = a * self.d + b
                row = self.rows[a + 1, b + 1].astype(F32)
                tile = jnp.where(lane == r, row[:, 0:1], tile)
                tile = jnp.where(lane == lanes // 2 + r, row[:, self.h - 1 : self.h], tile)
        self.own[...] = tile.astype(BF)

    def copies(self, build=True):
        place = {name: lax.axis_index(name) for name in AXES}
        size = {name: lax.axis_size(name) for name in AXES}

        def choices(name):
            i, n = place[name], size[name]
            if n == 1:
                return [(0, 0, True, True)]
            if n == 2:
                return [(0, 0, True, True), (1, 1 - 2 * i, True, True)]
            return [(0, 0, True, True), (1, 1, i < n - 1, i > 0), (2, -1, i > 0, i < n - 1)]

        def cells(step, code, count):
            if code == 0:
                return pl.ds(1, count), pl.ds(1, count)
            up = (1 + step) // 2
            return pl.ds(1 + (count - 1) * up, 1), pl.ds((count + 1) * (1 - up), 1)

        out = []
        for cw, sw, ow, iw in choices("wid"):
            for cd, sd, od, id_ in choices("dep"):
                for ch, sh, oh, ih in choices("hgt"):
                    if cw == 0 and cd == 0 and ch == 0:
                        continue
                    slot = self.index * 27 + (cw * 3 + cd) * 3 + ch
                    target = {"wid": place["wid"] + sw, "dep": place["dep"] + sd, "hgt": place["hgt"] + sh}
                    if not build:
                        out.append((target, [c for c in (ow, od, oh) if c is not True], [c for c in (iw, id_, ih) if c is not True]))
                        continue
                    if ch == 0:
                        from_w, to_w = cells(sw, cw, self.w)
                        from_d, to_d = cells(sd, cd, self.d)
                        source = self.rows.at[from_w, from_d]
                        dest = self.rows.at[to_w, to_d]
                    else:
                        source = self.own
                        dest = self.edges.at[(1 - sh) // 2, 1 - sw, 1 - sd]
                    copy = pltpu.make_async_remote_copy(
                        src_ref=source,
                        dst_ref=dest,
                        send_sem=self.send.at[slot],
                        recv_sem=self.recv.at[slot],
                        device_id=target,
                        device_id_type=pl.DeviceIdType.MESH,
                    )
                    out.append((copy, [c for c in (ow, od, oh) if c is not True], [c for c in (iw, id_, ih) if c is not True]))
        return out

    @staticmethod
    def guarded(conditions, action):
        if not conditions:
            action()
        else:
            pl.when(functools.reduce(jnp.logical_and, conditions))(action)

    def start(self):
        self.fill_edges()
        for copy, can_send, _ in self.copies():
            self.guarded(can_send, copy.start)

    def wait(self):
        for copy, _, can_take in self.copies():
            self.guarded(can_take, copy.wait_recv)

    def finish(self):
        for copy, can_send, _ in self.copies():
            self.guarded(can_send, copy.wait_send)

    def shifted(self, a, b, spread=None, fine=None):
        lanes = self.own.shape[1]
        h = self.h if spread is None else 2 * self.h
        row = self.rows[a, b]
        if spread is not None:
            row = mm(row, spread).astype(BF)
        dw = 0 if a == 0 else 2 if a == self.w + 1 else 1
        dd = 0 if b == 0 else 2 if b == self.d + 1 else 1
        r = (self.w - 1, a - 1, 0)[dw] * self.d + (self.d - 1, b - 1, 0)[dd]
        left = self.edges[0, dw, dd].astype(F32)[:, lanes // 2 + r : lanes // 2 + r + 1]
        right = self.edges[1, dw, dd].astype(F32)[:, r : r + 1]
        lane = lax.broadcasted_iota(jnp.int32, row.shape, 1)
        wide = row.astype(F32)
        before = jnp.where(lane == 0, left, pltpu.roll(wide, 1, 1))
        after = jnp.where(lane == h - 1, right, pltpu.roll(wide, lanes - 1, 1))
        if h < lanes:
            before = jnp.where(lane < h, before, 0.0)
            after = jnp.where(lane < h, after, 0.0)
        return before.astype(BF), row, after.astype(BF)


def at(name, position):
    return {n: position if n == name else lax.axis_index(n) for n in ("dep", "hgt", "wid")}


class Summed:
    order = ("wid", "hgt", "dep")

    def __init__(self, full, buffers, send, recv):
        self.total = buffers[0]
        self.levels = [(buffers[0], buffers[1], buffers[2]), buffers[3:6], buffers[6:9]]
        self.full, self.send, self.recv = full, send, recv
        self.stage, self.open, self.sent = 0, [], []

    def exchange(self, stage, name, pieces):
        i, n = lax.axis_index(name), lax.axis_size(name)
        self.open = []
        for k in range(1, n):
            source, dest = pieces(lax.rem(i + k, n), i)
            copy = pltpu.make_async_remote_copy(
                src_ref=source,
                dst_ref=dest,
                send_sem=self.send.at[stage, k],
                recv_sem=self.recv.at[stage, k],
                device_id=at(name, lax.rem(i + k, n)),
                device_id_type=pl.DeviceIdType.MESH,
            )
            copy.start()
            self.open.append(copy)
            self.sent.append(copy)

    def arrive(self):
        for copy in self.open:
            copy.wait_recv()
        self.open = []

    def step(self):
        stage = self.stage
        self.stage += 1
        if stage > 0:
            self.arrive()
        if 0 < stage <= 3:
            name = self.order[stage - 1]
            i, n = lax.axis_index(name), lax.axis_size(name)
            held, _, came = self.levels[stage - 1]
            m = held.shape[0] // n
            value = held[part(i, m)]
            for k in range(1, n):
                value = value + came[part(lax.rem(i + k, n), m)].astype(F32)
            if stage < 3:
                self.levels[stage][0][...] = value
            else:
                place = 0
                for axis in self.order:
                    place = place * lax.axis_size(axis) + lax.axis_index(axis)
                self.full[part(place, m)] = value.astype(BF)
        if stage < 3:
            held, wire, came = self.levels[stage]
            m = held.shape[0] // lax.axis_size(self.order[stage])
            wire[...] = held[...].astype(BF)
            self.exchange(stage, self.order[stage], lambda to, me: (wire.at[part(to, m)], came.at[part(me, m)]))
        elif stage < 6:
            depth = 6 - stage
            place, count = 0, 1
            for axis in self.order[:depth]:
                place = place * lax.axis_size(axis) + lax.axis_index(axis)
                count *= lax.axis_size(axis)
            m = self.full.shape[0] // count
            piece = self.full.at[part(place, m)]
            self.exchange(stage, self.order[depth - 1], lambda to, me: (piece, piece))

    def finish(self):
        while self.stage < 7:
            self.step()
        for copy in self.sent:
            copy.wait_send()


def part(i, m):
    return pl.ds(pl.multiple_of(i * m, 16), m)


def step_kernel(cfg, *refs):
    (f0, f1, f2, w, d, h) = cfg
    (feat, cot, raw_stem, raw_mid, raw_bot, w_rise, w_fin, b_rise, b_fin) = refs[:9]
    (output, full0, full1, full2, half_out) = refs[9:14]
    names = ("feat", "cot", "stem", "half", "mid", "quarter", "deep", "ra", "rg", "dg", "mg")
    refs = refs[14:]
    spans = {0: (w, d, h), 1: (w // 2, d // 2, h // 2), 2: (w // 4, d // 4, h // 4)}
    levels = dict(feat=0, cot=0, stem=0, half=1, mid=1, quarter=2, deep=2, ra=1, rg=1, dg=2, mg=1)
    send, recv = refs[0], refs[1]
    halo = {}
    for i, name in enumerate(names):
        rows, edges, own = refs[2 + 3 * i : 5 + 3 * i]
        halo[name] = Halo(i, rows, edges, own, spans[levels[name]], (send, recv))
    rest = refs[2 + 3 * len(names) :]
    (s_feat, s_cot, s_half, s_quarter, s_rise, s_fin, s_rg, s_dg, s_mg) = rest[:9]
    (stem_pre, mid_pre, deep_pre, rise_pre, fb_pool, fb_skip, rb_skip, stem_grad) = rest[9:17]
    (w_stem, w_mid, w_bot, b_mid, b_bot) = rest[17:22]
    rest = rest[22:]
    sums = [
        Summed(full, rest[11 * i : 11 * i + 9], rest[11 * i + 9], rest[11 * i + 10])
        for i, full in enumerate((full0, full1, full2))
    ]

    for item in halo.values():
        item.rows[...] = jnp.zeros(item.rows.shape, BF)
        item.edges[...] = jnp.zeros(item.edges.shape, BF)
    for a in range(w):
        for b in range(d):
            halo["feat"].rows[a + 1, b + 1] = feat[a, b]
            halo["cot"].rows[a + 1, b + 1] = cot[a, b]

    barrier = pltpu.get_barrier_semaphore()
    for target, can_send, _ in halo["feat"].copies(False):
        Halo.guarded(
            can_send,
            functools.partial(
                pl.semaphore_signal, barrier, 1, device_id=target, device_id_type=pl.DeviceIdType.MESH
            ),
        )
    others = 0
    for name in ("dep", "hgt"):
        i, n = lax.axis_index(name), lax.axis_size(name)
        for k in range(1, n):
            other = lax.rem(i + k, n)
            far = jnp.logical_or(other - i > 1, i - other > 1)
            if n > 2:
                Halo.guarded(
                    [far],
                    functools.partial(
                        pl.semaphore_signal, barrier, 1, device_id=at(name, other), device_id_type=pl.DeviceIdType.MESH
                    ),
                )
        others = others + n - (1 + jnp.minimum(i, 1) + jnp.minimum(n - 1 - i, 1))
    peers = 1
    for name in ("wid", "dep", "hgt"):
        i, n = lax.axis_index(name), lax.axis_size(name)
        peers = peers * (1 + jnp.minimum(i, 1) + jnp.minimum(n - 1 - i, 1))
    pl.semaphore_wait(barrier, peers - 1 + others)

    lanes = h
    pool = pattern(lanes, lambda r, c: r // 2 == c)
    pool_mean = (pool / 8.0).astype(BF)
    pool_sum = pool.astype(BF)
    spread = pattern(lanes, lambda r, c: c // 2 == r)
    spread_mean = (spread / 8.0).astype(BF)
    spread = spread.astype(BF)

    def stack_shifts(name, target):
        item = halo[name]
        for a in range(item.w + 2):
            for b in range(item.d + 2):
                target[a, b] = jnp.concatenate(item.shifted(a, b), axis=0)

    def stack_pair(coarse, fine, target):
        up, low = halo[coarse], halo[fine]
        for a in range(low.w + 2):
            for b in range(low.d + 2):
                one = up.shifted((a + 1) // 2, (b + 1) // 2, spread)
                two = low.shifted(a, b)
                target[a, b] = jnp.concatenate([v for pair in zip(one, two) for v in pair], axis=0)

    def patch(source, a, b, pair):
        parts = []
        for q in range(pair):
            parts.append(
                jnp.concatenate([source[a + ka, b + kb + q] for ka in range(3) for kb in range(3)], axis=0)
            )
        return parts[0] if pair == 1 else jnp.concatenate(parts, axis=1)

    def over_rows(span, body):
        pair = 2 if span[1] % 2 == 0 else 1
        across = span[1] // pair

        def trip(i, _):
            body(i // across, (i % across) * pair, pair)
            return 0

        count = span[0] * across
        if count == 1:
            body(0, 0, pair)
        else:
            lax.fori_loop(0, count, trip, 0)

    def conv(source, weight, span, store):
        def body(a, b, pair):
            result = mm(weight[...], patch(source, a, b, pair))
            for q in range(pair):
                store(a, b + q, result[:, q * lanes : (q + 1) * lanes])

        over_rows(span, body)

    def wgrad_into(base, patches, grad, width):
        groups = lanes // width
        count = patches.shape[0] // groups
        for g in range(groups):
            pieces = [jnp.zeros_like(grad)] * groups
            pieces[g] = grad
            full = pieces[0] if groups == 1 else jnp.concatenate(pieces, axis=0)
            value = mm_nt(patches[g * count : (g + 1) * count], full)
            where = sums[base[0]].total
            where[base[1] : base[1] + count] += value

    def grad_row(ref, a, b, pair, pad):
        parts = [ref[a + pad, b + pad + q] for q in range(pair)]
        return parts[0] if pair == 1 else jnp.concatenate(parts, axis=1)

    sizes = [27 * f0 * f0, 27 * f0 * f1, 27 * f1 * f2, 27 * (f2 + f1) * f1, 27 * (f1 + f0) * f0]
    rows_of = [v // lanes for v in sizes]
    bases = {i: (seg, sum(rows_of[j] for j in SEGMENTS[seg][: SEGMENTS[seg].index(i)])) for seg in range(3) for i in SEGMENTS[seg]}
    for item in sums:
        item.total[...] = jnp.zeros(item.total.shape, F32)

    halo["feat"].start()
    halo["cot"].start()
    for raw, target in ((raw_stem, w_stem), (raw_mid, w_mid), (raw_bot, w_bot)):
        target[...] = raw[...].reshape(-1, raw.shape[2]).T
    for raw, target in ((raw_mid, b_mid), (raw_bot, b_bot)):
        taps, _, width = raw.shape
        for k in range(taps):
            target[:, k * width : (k + 1) * width] = raw[taps - 1 - k]
    halo["feat"].wait()
    stack_shifts("feat", s_feat)

    def stem_store(a, b, value):
        stem_pre[a, b] = value
        halo["stem"].rows[a + 1, b + 1] = silu(value).astype(BF)

    conv(s_feat, w_stem, spans[0], stem_store)

    def pooled(fine, coarse):
        low, up = halo[fine], halo[coarse]
        for a in range(up.w):
            for b in range(up.d):
                cat = [low.rows[2 * a + 1 + i, 2 * b + 1 + j] for i in range(2) for j in range(2)]
                total = mm(cat[0], pool_mean) + mm(cat[1], pool_mean) + mm(cat[2], pool_mean) + mm(cat[3], pool_mean)
                up.rows[a + 1, b + 1] = total.astype(BF)

    pooled("stem", "half")
    halo["half"].start()
    halo["stem"].start()
    halo["cot"].wait()
    stack_shifts("cot", s_cot)
    fb_pool[...] = jnp.zeros(fb_pool.shape, F32)

    def back_store(a, b, value):
        fb_pool[a // 2, b // 2] += value[:f1]
        fb_skip[a, b] = value[f1:]

    conv(s_cot, b_fin, spans[0], back_store)
    halo["half"].wait()
    stack_shifts("half", s_half)

    def mid_store(a, b, value):
        mid_pre[a, b] = value
        halo["mid"].rows[a + 1, b + 1] = silu(value).astype(BF)

    conv(s_half, w_mid, spans[1], mid_store)
    pooled("mid", "quarter")
    halo["quarter"].start()
    halo["mid"].start()
    halo["quarter"].wait()
    stack_shifts("quarter", s_quarter)

    def deep_store(a, b, value):
        deep_pre[a, b] = value
        halo["deep"].rows[a + 1, b + 1] = silu(value).astype(BF)

    conv(s_quarter, w_bot, spans[2], deep_store)
    halo["deep"].start()
    halo["mid"].wait()
    halo["deep"].wait()
    stack_pair("deep", "mid", s_rise)

    def rise_store(a, b, value):
        rise_pre[a, b] = value
        halo["ra"].rows[a + 1, b + 1] = silu(value).astype(BF)
        grad = mm_split(fb_pool[a, b], pool_sum) * slope(value)
        halo["rg"].rows[a + 1, b + 1] = grad.astype(BF)

    conv(s_rise, w_rise, spans[1], rise_store)
    halo["rg"].start()
    halo["ra"].start()

    def rise_wgrad(a, b, pair):
        wgrad_into(bases[3], patch(s_rise, a, b, pair), grad_row(halo["rg"].rows, a, b, pair, 1), f1)

    over_rows(spans[1], rise_wgrad)
    sums[0].step()
    halo["rg"].wait()
    stack_shifts("rg", s_rg)
    deep_sum = [[None] * spans[2][1] for _ in range(spans[2][0])]

    pair1 = 2 if spans[1][1] % 2 == 0 else 1
    for a in range(spans[1][0]):
        for b in range(0, spans[1][1], pair1):
            result = mm(b_rise[...], patch(s_rg, a, b, pair1))
            for q in range(pair1):
                value = result[:, q * lanes : (q + 1) * lanes]
                rb_skip[a, b + q] = value[f2:]
                ap, bt = a // 2, (b + q) // 2
                old = deep_sum[ap][bt]
                deep_sum[ap][bt] = value[:f2] if old is None else old + value[:f2]
    for a in range(spans[2][0]):
        for b in range(spans[2][1]):
            grad = mm_split(deep_sum[a][b], pool_sum) * slope(deep_pre[a, b])
            halo["dg"].rows[a + 1, b + 1] = grad.astype(BF)
    halo["dg"].start()

    def bottom_wgrad(a, b, pair):
        wgrad_into(bases[2], patch(s_quarter, a, b, pair), grad_row(halo["dg"].rows, a, b, pair, 1), f2)

    over_rows(spans[2], bottom_wgrad)
    sums[0].step()
    halo["stem"].wait()
    halo["ra"].wait()
    stack_pair("ra", "stem", s_fin)

    def final(a, b, pair):
        cells = patch(s_fin, a, b, pair)
        result = mm(w_fin[...], cells)
        for q in range(pair):
            output[a, b + q] = result[:, q * lanes : (q + 1) * lanes].astype(BF)
        wgrad_into(bases[4], cells, grad_row(cot, a, b, pair, 0), f0)

    over_rows(spans[0], final)
    sums[1].step()
    sums[0].step()
    halo["dg"].wait()
    stack_shifts("dg", s_dg)

    def quarter_store(a, b, value):
        wide = mm_split(value, spread_mean)
        for i in range(2):
            for j in range(2):
                at_, bt = 2 * a + i, 2 * b + j
                grad = (rb_skip[at_, bt] + wide) * slope(mid_pre[at_, bt])
                halo["mg"].rows[at_ + 1, bt + 1] = grad.astype(BF)

    conv(s_dg, b_bot, spans[2], quarter_store)
    halo["mg"].start()
    sums[1].step()
    sums[0].step()

    def mid_wgrad(a, b, pair):
        wgrad_into(bases[1], patch(s_half, a, b, pair), grad_row(halo["mg"].rows, a, b, pair, 1), f1)

    over_rows(spans[1], mid_wgrad)
    sums[1].step()
    sums[0].step()
    halo["mg"].wait()
    stack_shifts("mg", s_mg)

    def half_store(a, b, value):
        half_out[a, b] = value
        wide = mm_split(value, spread_mean)
        for i in range(2):
            for j in range(2):
                at_, bt = 2 * a + i, 2 * b + j
                grad = (fb_skip[at_, bt] + wide) * slope(stem_pre[at_, bt])
                stem_grad[at_, bt] = grad.astype(BF)

    conv(s_mg, b_mid, spans[1], half_store)
    sums[1].step()
    sums[0].step()

    def stem_wgrad(a, b, pair):
        wgrad_into(bases[0], patch(s_feat, a, b, pair), grad_row(stem_grad, a, b, pair, 0), f0)

    over_rows(spans[0], stem_wgrad)
    sums[2].step()
    sums[0].step()
    sums[1].step()
    sums[2].step()
    sums[1].step()
    sums[2].step()
    sums[1].step()
    for item in (sums[2], sums[0], sums[1]):
        item.finish()
    for item in halo.values():
        item.finish()


def local(features, cotangent, w_stem, w_middle, w_bottom, w_rise, w_final):
    f0, w, d, h = features.shape
    f1, f2 = w_middle.shape[4], w_bottom.shape[4]
    spans = {0: (w, d), 1: (w // 2, d // 2), 2: (w // 4, d // 4)}
    halos = [(f0, 0), (f0, 0), (f0, 0), (f0, 1), (f1, 1), (f1, 2), (f2, 2), (f1, 1), (f1, 1), (f2, 2), (f1, 1)]
    scratch = [pltpu.SemaphoreType.DMA((27 * len(halos),)), pltpu.SemaphoreType.DMA((27 * len(halos),))]
    for c, level in halos:
        a, b = spans[level]
        scratch += [
            pltpu.VMEM((a + 2, b + 2, c, h), BF),
            pltpu.VMEM((2, 3, 3, c, h), BF),
            pltpu.VMEM((c, h), BF),
        ]
    for c, level in [(f0, 0), (f0, 0), (f0, 1), (f1, 2), (f2 + f1, 1), (f1 + f0, 0), (f1, 1), (f2, 2), (f1, 1)]:
        a, b = spans[level]
        scratch.append(pltpu.VMEM((a + 2, b + 2, 3 * c, h), BF))
    for c, level in [(f0, 0), (f1, 1), (f2, 2), (f1, 1), (f1, 1), (f0, 0), (f1, 1)]:
        scratch.append(pltpu.VMEM((*spans[level], c, h), F32))
    scratch.append(pltpu.VMEM((w, d, f0, h), BF))
    for a, b in ((f0, f0), (f1, f0), (f2, f1), (f0, f1), (f1, f2)):
        scratch.append(pltpu.VMEM((a, 27 * b), BF))
    weights = (w_stem, w_middle, w_bottom, w_rise, w_final)
    counts = [lax.axis_size(axis) for axis in Summed.order]
    unit = 16 * math.prod(counts)
    lengths = []
    for members in SEGMENTS:
        rows = -(-sum(weights[i].size // h for i in members) // unit) * unit
        lengths.append(rows)
        for n in counts:
            scratch += [pltpu.VMEM((rows, h), F32), pltpu.VMEM((rows, h), BF), pltpu.VMEM((rows, h), BF)]
            rows //= n
        scratch += [pltpu.SemaphoreType.DMA((6, max(counts))), pltpu.SemaphoreType.DMA((6, max(counts)))]

    def forward(v):
        return v.reshape(-1, v.shape[4]).T

    def backward(v):
        return v[::-1, ::-1, ::-1].reshape(27, v.shape[3], v.shape[4]).transpose(1, 0, 2).reshape(v.shape[3], -1)

    vmem = pl.BlockSpec(memory_space=pltpu.VMEM)
    out, *packed, half_back = pl.pallas_call(
        functools.partial(step_kernel, (f0, f1, f2, w, d, h)),
        out_shape=(
            jax.ShapeDtypeStruct((w, d, f0, h), BF),
            *[jax.ShapeDtypeStruct((rows, h), BF) for rows in lengths],
            jax.ShapeDtypeStruct((w // 2, d // 2, f0, h), F32),
        ),
        in_specs=[vmem] * 9,
        out_specs=(vmem,) * 5,
        scratch_shapes=scratch,
        compiler_params=pltpu.CompilerParams(
            collective_id=0, has_side_effects=True, vmem_limit_bytes=60 << 20
        ),
        name="unet_step",
    )(
        features.transpose(1, 2, 0, 3),
        cotangent.transpose(1, 2, 0, 3),
        *[v.reshape(-1, *v.shape[3:]) for v in weights[:3]],
        *[forward(v) for v in weights[3:]],
        *[backward(v) for v in weights[3:]],
    )
    cells = w * d * h * lax.axis_size("dep") * lax.axis_size("hgt") * lax.axis_size("wid")
    fine, mid, deep = (1.0 / math.sqrt(cells / k) for k in (1.0, 8.0, 64.0))
    scales = (fine, mid, deep, mid, fine)

    def unpack(*refs):
        for members, source in zip(SEGMENTS, refs[:3]):
            base = 0
            for i in members:
                target = refs[3 + i]
                width = target.shape[1]
                rows = target.shape[0] * width // h
                value = source[base : base + rows].astype(F32) * scales[i]
                base += rows
                for g in range(h // width):
                    target[g * rows : (g + 1) * rows] = value[:, g * width : (g + 1) * width]

    flat = pl.pallas_call(
        unpack,
        out_shape=tuple(jax.ShapeDtypeStruct((v.size // v.shape[4], v.shape[4]), F32) for v in weights),
        in_specs=[vmem] * 3,
        out_specs=(vmem,) * 5,
        compiler_params=pltpu.CompilerParams(vmem_limit_bytes=32 << 20),
        name="unpack",
    )(*packed)
    results = [r.reshape(v.shape) for r, v in zip(flat, weights)]
    return (out.transpose(2, 0, 1, 3), *results, half_back[..., : h // 2].transpose(2, 0, 1, 3))


def solution(mesh):
    placed = (P("grp", "wid", "dep", "hgt"), P("grp", "wid", "dep", "hgt"), P(), P(), P(), P(), P())
    grad = P("grp", None, None, None, None)
    return jax.shard_map(
        local,
        mesh=mesh,
        in_specs=placed,
        out_specs=(P("grp", "wid", "dep", "hgt"), grad, grad, grad, grad, grad, P("grp", "wid", "dep", "hgt")),
        check_vma=False,
    )
```

```python
import functools
import math

import jax
import jax.numpy as jnp
from jax import lax
from jax.experimental import pallas as pl
from jax.experimental.pallas import tpu as pltpu
from jax.sharding import PartitionSpec as P

BF, F32 = jnp.bfloat16, jnp.float32
SEGMENTS = ((3,), (2, 4), (1, 0))
AXES = ("grp", "dep", "hgt", "wid")


def mm(a, b):
    return lax.dot_general(a, b, (((1,), (0,)), ((), ())), preferred_element_type=F32)


def mm_nt(a, b):
    return lax.dot_general(a, b, (((1,), (1,)), ((), ())), preferred_element_type=F32)


def mm_split(a, b):
    high = a.astype(BF)
    low = (a - high.astype(F32)).astype(BF)
    return mm(high, b) + mm(low, b)


def silu(v):
    return v * jax.nn.sigmoid(v)


def slope(v):
    g = jax.nn.sigmoid(v)
    return g * (1.0 + v * (1.0 - g))


def pattern(lanes, test):
    row = lax.broadcasted_iota(jnp.int32, (lanes, lanes), 0)
    col = lax.broadcasted_iota(jnp.int32, (lanes, lanes), 1)
    return jnp.where(test(row, col), 1.0, 0.0)


class Halo:
    def __init__(self, index, rows, edges, own, span, sems):
        self.index, self.rows, self.edges, self.own = index, rows, edges, own
        self.w, self.d, self.h = span
        self.send, self.recv = sems

    def fill_edges(self):
        lanes = self.own.shape[1]
        lane = lax.broadcasted_iota(jnp.int32, self.own.shape, 1)
        tile = jnp.zeros(self.own.shape, F32)
        for a in range(self.w):
            for b in range(self.d):
                r = a * self.d + b
                row = self.rows[a + 1, b + 1].astype(F32)
                tile = jnp.where(lane == r, row[:, 0:1], tile)
                tile = jnp.where(lane == lanes // 2 + r, row[:, self.h - 1 : self.h], tile)
        self.own[...] = tile.astype(BF)

    def copies(self, build=True):
        place = {name: lax.axis_index(name) for name in AXES}
        size = {name: lax.axis_size(name) for name in AXES}

        def choices(name):
            i, n = place[name], size[name]
            if n == 1:
                return [(0, 0, True, True)]
            if n == 2:
                return [(0, 0, True, True), (1, 1 - 2 * i, True, True)]
            return [(0, 0, True, True), (1, 1, i < n - 1, i > 0), (2, -1, i > 0, i < n - 1)]

        def cells(step, code, count):
            if code == 0:
                return pl.ds(1, count), pl.ds(1, count)
            up = (1 + step) // 2
            return pl.ds(1 + (count - 1) * up, 1), pl.ds((count + 1) * (1 - up), 1)

        out = []
        for cw, sw, ow, iw in choices("wid"):
            for cd, sd, od, id_ in choices("dep"):
                for ch, sh, oh, ih in choices("hgt"):
                    if cw == 0 and cd == 0 and ch == 0:
                        continue
                    slot = self.index * 27 + (cw * 3 + cd) * 3 + ch
                    target = {"wid": place["wid"] + sw, "dep": place["dep"] + sd, "hgt": place["hgt"] + sh}
                    if not build:
                        out.append((target, [c for c in (ow, od, oh) if c is not True], [c for c in (iw, id_, ih) if c is not True]))
                        continue
                    if ch == 0:
                        from_w, to_w = cells(sw, cw, self.w)
                        from_d, to_d = cells(sd, cd, self.d)
                        source = self.rows.at[from_w, from_d]
                        dest = self.rows.at[to_w, to_d]
                    else:
                        source = self.own
                        dest = self.edges.at[(1 - sh) // 2, 1 - sw, 1 - sd]
                    copy = pltpu.make_async_remote_copy(
                        src_ref=source,
                        dst_ref=dest,
                        send_sem=self.send.at[slot],
                        recv_sem=self.recv.at[slot],
                        device_id=target,
                        device_id_type=pl.DeviceIdType.MESH,
                    )
                    out.append((copy, [c for c in (ow, od, oh) if c is not True], [c for c in (iw, id_, ih) if c is not True]))
        return out

    @staticmethod
    def guarded(conditions, action):
        if not conditions:
            action()
        else:
            pl.when(functools.reduce(jnp.logical_and, conditions))(action)

    def start(self):
        self.fill_edges()
        for copy, can_send, _ in self.copies():
            self.guarded(can_send, copy.start)

    def wait(self):
        for copy, _, can_take in self.copies():
            self.guarded(can_take, copy.wait_recv)

    def finish(self):
        for copy, can_send, _ in self.copies():
            self.guarded(can_send, copy.wait_send)

    def shifted(self, a, b, spread=None, fine=None):
        lanes = self.own.shape[1]
        h = self.h if spread is None else 2 * self.h
        row = self.rows[a, b]
        if spread is not None:
            row = mm(row, spread).astype(BF)
        dw = 0 if a == 0 else 2 if a == self.w + 1 else 1
        dd = 0 if b == 0 else 2 if b == self.d + 1 else 1
        r = (self.w - 1, a - 1, 0)[dw] * self.d + (self.d - 1, b - 1, 0)[dd]
        left = self.edges[0, dw, dd].astype(F32)[:, lanes // 2 + r : lanes // 2 + r + 1]
        right = self.edges[1, dw, dd].astype(F32)[:, r : r + 1]
        lane = lax.broadcasted_iota(jnp.int32, row.shape, 1)
        wide = row.astype(F32)
        before = jnp.where(lane == 0, left, pltpu.roll(wide, 1, 1))
        after = jnp.where(lane == h - 1, right, pltpu.roll(wide, lanes - 1, 1))
        if h < lanes:
            before = jnp.where(lane < h, before, 0.0)
            after = jnp.where(lane < h, after, 0.0)
        return before.astype(BF), row, after.astype(BF)


def at(name, position):
    return {n: position if n == name else lax.axis_index(n) for n in ("dep", "hgt", "wid")}


class Summed:
    order = ("wid", "hgt", "dep")

    def __init__(self, full, buffers, send, recv):
        self.total = buffers[0]
        self.levels = [(buffers[0], buffers[1], buffers[2]), buffers[3:6], buffers[6:9]]
        self.full, self.send, self.recv = full, send, recv
        self.stage, self.open, self.sent = 0, [], []

    def exchange(self, stage, name, pieces):
        i, n = lax.axis_index(name), lax.axis_size(name)
        self.open = []
        for k in range(1, n):
            source, dest = pieces(lax.rem(i + k, n), i)
            copy = pltpu.make_async_remote_copy(
                src_ref=source,
                dst_ref=dest,
                send_sem=self.send.at[stage, k],
                recv_sem=self.recv.at[stage, k],
                device_id=at(name, lax.rem(i + k, n)),
                device_id_type=pl.DeviceIdType.MESH,
            )
            copy.start()
            self.open.append(copy)
            self.sent.append(copy)

    def arrive(self):
        for copy in self.open:
            copy.wait_recv()
        self.open = []

    def step(self):
        stage = self.stage
        self.stage += 1
        if stage > 0:
            self.arrive()
        if 0 < stage <= 3:
            name = self.order[stage - 1]
            i, n = lax.axis_index(name), lax.axis_size(name)
            held, _, came = self.levels[stage - 1]
            m = held.shape[0] // n
            value = held[part(i, m)]
            for k in range(1, n):
                value = value + came[part(lax.rem(i + k, n), m)].astype(F32)
            if stage < 3:
                self.levels[stage][0][...] = value
            else:
                place = 0
                for axis in self.order:
                    place = place * lax.axis_size(axis) + lax.axis_index(axis)
                self.full[part(place, m)] = value.astype(BF)
        if stage < 3:
            held, wire, came = self.levels[stage]
            m = held.shape[0] // lax.axis_size(self.order[stage])
            wire[...] = held[...].astype(BF)
            self.exchange(stage, self.order[stage], lambda to, me: (wire.at[part(to, m)], came.at[part(me, m)]))
        elif stage < 6:
            depth = 6 - stage
            place, count = 0, 1
            for axis in self.order[:depth]:
                place = place * lax.axis_size(axis) + lax.axis_index(axis)
                count *= lax.axis_size(axis)
            m = self.full.shape[0] // count
            piece = self.full.at[part(place, m)]
            self.exchange(stage, self.order[depth - 1], lambda to, me: (piece, piece))

    def finish(self):
        while self.stage < 7:
            self.step()
        for copy in self.sent:
            copy.wait_send()


def part(i, m):
    return pl.ds(pl.multiple_of(i * m, 16), m)


def step_kernel(cfg, *refs):
    (f0, f1, f2, w, d, h) = cfg
    (feat, cot, raw_stem, raw_mid, raw_bot, w_rise, w_fin, b_rise, b_fin) = refs[:9]
    (output, full0, full1, full2, half_out) = refs[9:14]
    names = ("feat", "cot", "stem", "half", "mid", "quarter", "deep", "ra", "rg", "dg", "mg")
    refs = refs[14:]
    spans = {0: (w, d, h), 1: (w // 2, d // 2, h // 2), 2: (w // 4, d // 4, h // 4)}
    levels = dict(feat=0, cot=0, stem=0, half=1, mid=1, quarter=2, deep=2, ra=1, rg=1, dg=2, mg=1)
    send, recv = refs[0], refs[1]
    halo = {}
    for i, name in enumerate(names):
        rows, edges, own = refs[2 + 3 * i : 5 + 3 * i]
        halo[name] = Halo(i, rows, edges, own, spans[levels[name]], (send, recv))
    rest = refs[2 + 3 * len(names) :]
    (s_feat, s_cot, s_half, s_quarter, s_rise, s_fin, s_rg, s_dg, s_mg) = rest[:9]
    (stem_pre, mid_pre, deep_pre, rise_pre, fb_pool, fb_skip, rb_skip, stem_grad) = rest[9:17]
    (w_stem, w_mid, w_bot, b_mid, b_bot) = rest[17:22]
    rest = rest[22:]
    sums = [
        Summed(full, rest[11 * i : 11 * i + 9], rest[11 * i + 9], rest[11 * i + 10])
        for i, full in enumerate((full0, full1, full2))
    ]

    for item in halo.values():
        item.rows[...] = jnp.zeros(item.rows.shape, BF)
        item.edges[...] = jnp.zeros(item.edges.shape, BF)
    for a in range(w):
        for b in range(d):
            halo["feat"].rows[a + 1, b + 1] = feat[a, b]
            halo["cot"].rows[a + 1, b + 1] = cot[a, b]

    barrier = pltpu.get_barrier_semaphore()
    for target, can_send, _ in halo["feat"].copies(False):
        Halo.guarded(
            can_send,
            functools.partial(
                pl.semaphore_signal, barrier, 1, device_id=target, device_id_type=pl.DeviceIdType.MESH
            ),
        )
    others = 0
    for name in ("dep", "hgt"):
        i, n = lax.axis_index(name), lax.axis_size(name)
        for k in range(1, n):
            other = lax.rem(i + k, n)
            far = jnp.logical_or(other - i > 1, i - other > 1)
            if n > 2:
                Halo.guarded(
                    [far],
                    functools.partial(
                        pl.semaphore_signal, barrier, 1, device_id=at(name, other), device_id_type=pl.DeviceIdType.MESH
                    ),
                )
        others = others + n - (1 + jnp.minimum(i, 1) + jnp.minimum(n - 1 - i, 1))
    peers = 1
    for name in ("wid", "dep", "hgt"):
        i, n = lax.axis_index(name), lax.axis_size(name)
        peers = peers * (1 + jnp.minimum(i, 1) + jnp.minimum(n - 1 - i, 1))
    pl.semaphore_wait(barrier, peers - 1 + others)

    lanes = h
    pool = pattern(lanes, lambda r, c: r // 2 == c)
    pool_mean = (pool / 8.0).astype(BF)
    pool_sum = pool.astype(BF)
    spread = pattern(lanes, lambda r, c: c // 2 == r)
    spread_mean = (spread / 8.0).astype(BF)
    spread = spread.astype(BF)

    def stack_shifts(name, target):
        item = halo[name]
        for a in range(item.w + 2):
            for b in range(item.d + 2):
                target[a, b] = jnp.concatenate(item.shifted(a, b), axis=0)

    def stack_pair(coarse, fine, target):
        up, low = halo[coarse], halo[fine]
        for a in range(low.w + 2):
            for b in range(low.d + 2):
                one = up.shifted((a + 1) // 2, (b + 1) // 2, spread)
                two = low.shifted(a, b)
                target[a, b] = jnp.concatenate([v for pair in zip(one, two) for v in pair], axis=0)

    def patch(source, a, b, pair):
        parts = []
        for q in range(pair):
            parts.append(
                jnp.concatenate([source[a + ka, b + kb + q] for ka in range(3) for kb in range(3)], axis=0)
            )
        return parts[0] if pair == 1 else jnp.concatenate(parts, axis=1)

    def over_rows(span, body):
        pair = 4 if span[1] % 4 == 0 else 2 if span[1] % 2 == 0 else 1
        across = span[1] // pair

        def trip(i, _):
            body(i // across, (i % across) * pair, pair)
            return 0

        count = span[0] * across
        if count == 1:
            body(0, 0, pair)
        else:
            lax.fori_loop(0, count, trip, 0)

    def conv(source, weight, span, store):
        def body(a, b, pair):
            result = mm(weight[...], patch(source, a, b, pair))
            for q in range(pair):
                store(a, b + q, result[:, q * lanes : (q + 1) * lanes])

        over_rows(span, body)

    def wgrad_into(base, patches, grad, width):
        groups = lanes // width
        count = patches.shape[0] // groups
        value = None
        for g in range(groups):
            pieces = [jnp.zeros_like(grad)] * groups
            pieces[g] = grad
            full = pieces[0] if groups == 1 else jnp.concatenate(pieces, axis=0)
            piece = mm_nt(patches[g * count : (g + 1) * count], full)
            value = piece if value is None else value + piece
        where = sums[base[0]].total
        where[base[1] : base[1] + count] += value

    def grad_row(ref, a, b, pair, pad):
        parts = [ref[a + pad, b + pad + q] for q in range(pair)]
        return parts[0] if pair == 1 else jnp.concatenate(parts, axis=1)

    sizes = [27 * f0 * f0, 27 * f0 * f1, 27 * f1 * f2, 27 * (f2 + f1) * f1, 27 * (f1 + f0) * f0]
    rows_of = [v // lanes for v in sizes]
    bases = {i: (seg, sum(rows_of[j] for j in SEGMENTS[seg][: SEGMENTS[seg].index(i)])) for seg in range(3) for i in SEGMENTS[seg]}
    for item in sums:
        item.total[...] = jnp.zeros(item.total.shape, F32)

    halo["feat"].start()
    halo["cot"].start()
    for raw, target in ((raw_stem, w_stem), (raw_mid, w_mid), (raw_bot, w_bot)):
        target[...] = raw[...].reshape(-1, raw.shape[2]).T
    for raw, target in ((raw_mid, b_mid), (raw_bot, b_bot)):
        taps, _, width = raw.shape
        for k in range(taps):
            target[:, k * width : (k + 1) * width] = raw[taps - 1 - k]
    halo["feat"].wait()
    stack_shifts("feat", s_feat)

    def stem_store(a, b, value):
        stem_pre[a, b] = value
        halo["stem"].rows[a + 1, b + 1] = silu(value).astype(BF)

    conv(s_feat, w_stem, spans[0], stem_store)

    def pooled(fine, coarse):
        low, up = halo[fine], halo[coarse]
        for a in range(up.w):
            for b in range(up.d):
                cat = [low.rows[2 * a + 1 + i, 2 * b + 1 + j] for i in range(2) for j in range(2)]
                total = mm(cat[0], pool_mean) + mm(cat[1], pool_mean) + mm(cat[2], pool_mean) + mm(cat[3], pool_mean)
                up.rows[a + 1, b + 1] = total.astype(BF)

    pooled("stem", "half")
    halo["half"].start()
    halo["stem"].start()
    halo["cot"].wait()
    stack_shifts("cot", s_cot)
    fb_pool[...] = jnp.zeros(fb_pool.shape, F32)

    def back_store(a, b, value):
        fb_pool[a // 2, b // 2] += value[:f1]
        fb_skip[a, b] = value[f1:]

    conv(s_cot, b_fin, spans[0], back_store)
    halo["half"].wait()
    stack_shifts("half", s_half)

    def mid_store(a, b, value):
        mid_pre[a, b] = value
        halo["mid"].rows[a + 1, b + 1] = silu(value).astype(BF)

    conv(s_half, w_mid, spans[1], mid_store)
    pooled("mid", "quarter")
    halo["quarter"].start()
    halo["mid"].start()
    halo["quarter"].wait()
    stack_shifts("quarter", s_quarter)

    def deep_store(a, b, value):
        deep_pre[a, b] = value
        halo["deep"].rows[a + 1, b + 1] = silu(value).astype(BF)

    conv(s_quarter, w_bot, spans[2], deep_store)
    halo["deep"].start()
    halo["mid"].wait()
    halo["deep"].wait()
    stack_pair("deep", "mid", s_rise)

    def rise_store(a, b, value):
        rise_pre[a, b] = value
        halo["ra"].rows[a + 1, b + 1] = silu(value).astype(BF)
        grad = mm_split(fb_pool[a, b], pool_sum) * slope(value)
        halo["rg"].rows[a + 1, b + 1] = grad.astype(BF)

    conv(s_rise, w_rise, spans[1], rise_store)
    halo["rg"].start()
    halo["ra"].start()

    def rise_wgrad(a, b, pair):
        wgrad_into(bases[3], patch(s_rise, a, b, pair), grad_row(halo["rg"].rows, a, b, pair, 1), f1)

    over_rows(spans[1], rise_wgrad)
    sums[0].step()
    halo["rg"].wait()
    stack_shifts("rg", s_rg)
    deep_sum = [[None] * spans[2][1] for _ in range(spans[2][0])]

    pair1 = 2 if spans[1][1] % 2 == 0 else 1
    for a in range(spans[1][0]):
        for b in range(0, spans[1][1], pair1):
            result = mm(b_rise[...], patch(s_rg, a, b, pair1))
            for q in range(pair1):
                value = result[:, q * lanes : (q + 1) * lanes]
                rb_skip[a, b + q] = value[f2:]
                ap, bt = a // 2, (b + q) // 2
                old = deep_sum[ap][bt]
                deep_sum[ap][bt] = value[:f2] if old is None else old + value[:f2]
    for a in range(spans[2][0]):
        for b in range(spans[2][1]):
            grad = mm_split(deep_sum[a][b], pool_sum) * slope(deep_pre[a, b])
            halo["dg"].rows[a + 1, b + 1] = grad.astype(BF)
    halo["dg"].start()

    def bottom_wgrad(a, b, pair):
        wgrad_into(bases[2], patch(s_quarter, a, b, pair), grad_row(halo["dg"].rows, a, b, pair, 1), f2)

    over_rows(spans[2], bottom_wgrad)
    sums[0].step()
    halo["stem"].wait()
    halo["ra"].wait()
    stack_pair("ra", "stem", s_fin)

    def final(a, b, pair):
        cells = patch(s_fin, a, b, pair)
        result = mm(w_fin[...], cells)
        for q in range(pair):
            output[a, b + q] = result[:, q * lanes : (q + 1) * lanes].astype(BF)
        wgrad_into(bases[4], cells, grad_row(cot, a, b, pair, 0), f0)

    over_rows(spans[0], final)
    sums[1].step()
    sums[0].step()
    halo["dg"].wait()
    stack_shifts("dg", s_dg)

    def quarter_store(a, b, value):
        wide = mm_split(value, spread_mean)
        for i in range(2):
            for j in range(2):
                at_, bt = 2 * a + i, 2 * b + j
                grad = (rb_skip[at_, bt] + wide) * slope(mid_pre[at_, bt])
                halo["mg"].rows[at_ + 1, bt + 1] = grad.astype(BF)

    conv(s_dg, b_bot, spans[2], quarter_store)
    halo["mg"].start()
    sums[1].step()
    sums[0].step()

    def mid_wgrad(a, b, pair):
        wgrad_into(bases[1], patch(s_half, a, b, pair), grad_row(halo["mg"].rows, a, b, pair, 1), f1)

    over_rows(spans[1], mid_wgrad)
    sums[1].step()
    sums[0].step()
    halo["mg"].wait()
    stack_shifts("mg", s_mg)

    def half_store(a, b, value):
        half_out[a, b] = value
        wide = mm_split(value, spread_mean)
        for i in range(2):
            for j in range(2):
                at_, bt = 2 * a + i, 2 * b + j
                grad = (fb_skip[at_, bt] + wide) * slope(stem_pre[at_, bt])
                stem_grad[at_, bt] = grad.astype(BF)

    conv(s_mg, b_mid, spans[1], half_store)
    sums[1].step()
    sums[0].step()

    def stem_wgrad(a, b, pair):
        wgrad_into(bases[0], patch(s_feat, a, b, pair), grad_row(stem_grad, a, b, pair, 0), f0)

    over_rows(spans[0], stem_wgrad)
    sums[2].step()
    sums[0].step()
    sums[1].step()
    sums[2].step()
    sums[1].step()
    sums[2].step()
    sums[1].step()
    for item in (sums[2], sums[0], sums[1]):
        item.finish()
    for item in halo.values():
        item.finish()


def local(features, cotangent, w_stem, w_middle, w_bottom, w_rise, w_final):
    f0, w, d, h = features.shape
    f1, f2 = w_middle.shape[4], w_bottom.shape[4]
    spans = {0: (w, d), 1: (w // 2, d // 2), 2: (w // 4, d // 4)}
    halos = [(f0, 0), (f0, 0), (f0, 0), (f0, 1), (f1, 1), (f1, 2), (f2, 2), (f1, 1), (f1, 1), (f2, 2), (f1, 1)]
    scratch = [pltpu.SemaphoreType.DMA((27 * len(halos),)), pltpu.SemaphoreType.DMA((27 * len(halos),))]
    for c, level in halos:
        a, b = spans[level]
        scratch += [
            pltpu.VMEM((a + 2, b + 2, c, h), BF),
            pltpu.VMEM((2, 3, 3, c, h), BF),
            pltpu.VMEM((c, h), BF),
        ]
    for c, level in [(f0, 0), (f0, 0), (f0, 1), (f1, 2), (f2 + f1, 1), (f1 + f0, 0), (f1, 1), (f2, 2), (f1, 1)]:
        a, b = spans[level]
        scratch.append(pltpu.VMEM((a + 2, b + 2, 3 * c, h), BF))
    for c, level in [(f0, 0), (f1, 1), (f2, 2), (f1, 1), (f1, 1), (f0, 0), (f1, 1)]:
        scratch.append(pltpu.VMEM((*spans[level], c, h), F32))
    scratch.append(pltpu.VMEM((w, d, f0, h), BF))
    for a, b in ((f0, f0), (f1, f0), (f2, f1), (f0, f1), (f1, f2)):
        scratch.append(pltpu.VMEM((a, 27 * b), BF))
    weights = (w_stem, w_middle, w_bottom, w_rise, w_final)
    counts = [lax.axis_size(axis) for axis in Summed.order]
    unit = 16 * math.prod(counts)
    lengths = []
    for members in SEGMENTS:
        rows = -(-sum(weights[i].size // h for i in members) // unit) * unit
        lengths.append(rows)
        for n in counts:
            scratch += [pltpu.VMEM((rows, h), F32), pltpu.VMEM((rows, h), BF), pltpu.VMEM((rows, h), BF)]
            rows //= n
        scratch += [pltpu.SemaphoreType.DMA((6, max(counts))), pltpu.SemaphoreType.DMA((6, max(counts)))]

    def forward(v):
        return v.reshape(-1, v.shape[4]).T

    def backward(v):
        return v[::-1, ::-1, ::-1].reshape(27, v.shape[3], v.shape[4]).transpose(1, 0, 2).reshape(v.shape[3], -1)

    vmem = pl.BlockSpec(memory_space=pltpu.VMEM)
    out, *packed, half_back = pl.pallas_call(
        functools.partial(step_kernel, (f0, f1, f2, w, d, h)),
        out_shape=(
            jax.ShapeDtypeStruct((w, d, f0, h), BF),
            *[jax.ShapeDtypeStruct((rows, h), BF) for rows in lengths],
            jax.ShapeDtypeStruct((w // 2, d // 2, f0, h), F32),
        ),
        in_specs=[vmem] * 9,
        out_specs=(vmem,) * 5,
        scratch_shapes=scratch,
        compiler_params=pltpu.CompilerParams(
            collective_id=0, has_side_effects=True, vmem_limit_bytes=60 << 20
        ),
        name="unet_step",
    )(
        features.transpose(1, 2, 0, 3),
        cotangent.transpose(1, 2, 0, 3),
        *[v.reshape(-1, *v.shape[3:]) for v in weights[:3]],
        *[forward(v) for v in weights[3:]],
        *[backward(v) for v in weights[3:]],
    )
    cells = w * d * h * lax.axis_size("dep") * lax.axis_size("hgt") * lax.axis_size("wid")
    fine, mid, deep = (1.0 / math.sqrt(cells / k) for k in (1.0, 8.0, 64.0))
    scales = (fine, mid, deep, mid, fine)

    def unpack(*refs):
        for members, source in zip(SEGMENTS, refs[:3]):
            base = 0
            for i in members:
                target = refs[3 + i]
                width = target.shape[1]
                rows = target.shape[0] * width // h
                value = source[base : base + rows].astype(F32) * scales[i]
                base += rows
                for g in range(h // width):
                    target[g * rows : (g + 1) * rows] = value[:, g * width : (g + 1) * width]

    flat = pl.pallas_call(
        unpack,
        out_shape=tuple(jax.ShapeDtypeStruct((v.size // v.shape[4], v.shape[4]), F32) for v in weights),
        in_specs=[vmem] * 3,
        out_specs=(vmem,) * 5,
        compiler_params=pltpu.CompilerParams(vmem_limit_bytes=32 << 20),
        name="unpack",
    )(*packed)
    results = [r.reshape(v.shape) for r, v in zip(flat, weights)]
    return (out.transpose(2, 0, 1, 3), *results, half_back[..., : h // 2].transpose(2, 0, 1, 3))


def solution(mesh):
    placed = (P("grp", "wid", "dep", "hgt"), P("grp", "wid", "dep", "hgt"), P(), P(), P(), P(), P())
    grad = P("grp", None, None, None, None)
    return jax.shard_map(
        local,
        mesh=mesh,
        in_specs=placed,
        out_specs=(P("grp", "wid", "dep", "hgt"), grad, grad, grad, grad, grad, P("grp", "wid", "dep", "hgt")),
        check_vma=False,
    )
```
